512 devices in a mesh: shard: 64 (over x, z, core), rep: 8 (over y).
Axes of the slice: x: 4, y: 8, z: 8, core: 2. Of those that a mesh axis runs over, the one named last changes fastest.
Arguments:
- attn_grad: bfloat16 [8, 2, 4, 768, 768], P('rep', None, None, 'shard'), may hold values from -16 to 16
- attn_error: float32 [8, 2, 4, 768, 768], P('rep', None, None, 'shard'), may hold values from -6 to 6
- attn_basis: float32 [2, 4, 768, 32], P(None, None, 'shard'), may hold values from -0.21875 to 0.21875
- attn_roots: float32 [2, 4, 3, 32, 32], replicated, as said below
- attn_momentum: float32 [2, 4, 768, 768], P(None, None, 'shard'), may hold values from -4 to 4
- attn_weights: float32 [2, 4, 768, 768], P(None, None, 'shard'), may hold values from -0.21875 to 0.21875
- mlp_grad: bfloat16 [8, 2, 2, 768, 3072], P('rep', None, None, 'shard'), may hold values from -16 to 16
- mlp_error: float32 [8, 2, 2, 768, 3072], P('rep', None, None, 'shard'), may hold values from -6 to 6
- mlp_basis: float32 [2, 2, 3072, 32], P(None, None, 'shard'), may hold values from -0.109375 to 0.109375
- mlp_roots: float32 [2, 2, 3, 32, 32], replicated, as said below
- mlp_momentum: float32 [2, 2, 768, 3072], P(None, None, 'shard'), may hold values from -4 to 4
- mlp_weights: float32 [2, 2, 768, 3072], P(None, None, 'shard'), may hold values from -0.21875 to 0.21875
- small_grad: bfloat16 [8, 2, 9984], P('rep', None, 'shard'), may hold values from -6 to 6
- small_momentum: float32 [2, 9984], P(None, 'shard'), may hold values from -4 to 4
- small_weights: float32 [2, 9984], P(None, 'shard'), may hold values from -6 to 6
Outputs:
- attn_error_out: float32 [8, 2, 4, 768, 768], P('rep', None, None, 'shard')
- mlp_error_out: float32 [8, 2, 2, 768, 3072], P('rep', None, None, 'shard')
- attn_left: float32 [2, 4, 768, 32], P(None, None, 'shard')
- attn_right: float32 [2, 4, 768, 32], P(None, None, 'shard')
- mlp_left: float32 [2, 2, 768, 32], P(None, None, 'shard')
- mlp_right: float32 [2, 2, 3072, 32], P(None, None, 'shard')
- attn_momentum_out: float32 [2, 4, 768, 768], P(None, None, 'shard')
- attn_weights_out: float32 [2, 4, 768, 768], P(None, None, 'shard')
- mlp_momentum_out: float32 [2, 2, 768, 3072], P(None, None, 'shard')
- mlp_weights_out: float32 [2, 2, 768, 3072], P(None, None, 'shard')
- small_momentum_out: float32 [2, 9984], P(None, 'shard')
- small_weights_out: float32 [2, 9984], P(None, 'shard')
The draws below stay inside these ranges and needn't reach their ends.
Inputs may be any that keep to these rules, and one draw needn't show every extreme that they name: Every 32 x 32 factor of attn_roots is a scaled identity plus independent entries and is well conditioned. Every 32 x 32 factor of mlp_roots is a scaled identity plus independent entries and is well conditioned.
All inputs are finite; a program needn't handle non-finite values.
Results may differ from the reference program's by a relative error of at most 0.0003.
Values sent between devices are 32-bit elements; how exact they have to be, the bound alone decides.
A program may use at most 64 MiB of HBM per device.

```python
import math
import jax
import jax.numpy as jnp
from jax import lax

D = 768
FF = 3072
LAYERS = 2
RANK = 32
VEC = 9984
N_REP = 8


def root_factors(key, count, columns):
    shape = (LAYERS, count, 3, RANK, RANK)
    noise = 0.06 * jax.random.normal(key, shape, jnp.float32)
    identity = jnp.eye(RANK, dtype=jnp.float32)
    scales = jnp.array([0.25 / math.sqrt(D), 0.25 / math.sqrt(columns), 0.25 * D ** (-0.25)], jnp.float32)
    return (identity + noise) * scales[None, None, :, None, None]


def draw_attn_roots(key, part):
    return root_factors(jax.random.fold_in(key, 11), 4, D)


def draw_mlp_roots(key, part):
    return root_factors(jax.random.fold_in(key, 23), 2, FF)


def strengthened(values, rng, source, target, shards_of, factor):
    owner, partner = [(jnp.arange(values.shape[position]) // (values.shape[position] // shards_of)).reshape([-1 if axis == position else 1 for axis in range(values.ndim)]) for position in (source, target)]
    chosen = jax.random.permutation(rng, shards_of)[partner]
    strong = (owner == chosen) | (owner == (partner + shards_of // 2) % shards_of)
    return jnp.where(strong, factor * values, values)


def steps_of(key, shape, pieces, low, largest):
    factor_of, own = 1.0, jax.random.fold_in(key, 6)
    for position, parts in pieces:
        draws = jnp.exp(jax.random.uniform(jax.random.fold_in(own, position), (parts,), jnp.float32, low / len(pieces), largest / len(pieces)))
        factor_of = factor_of * jnp.repeat(draws, shape[position] // parts).reshape([-1 if axis == position else 1 for axis in range(len(shape))])
    return factor_of


def gaussian(key, shape, spread, bound, pieces=(), held_as=jnp.bfloat16):
    values = jax.random.normal(key, shape, jnp.float32) * spread
    if len(pieces) > 0:
        values = steps_of(key, shape, pieces, -0.22, 0.18) * values
    return jnp.clip(values, min=-bound, max=bound).astype(held_as)


def gaussian_with(rng, shape, scale, reach, shards, heavy, kind=jnp.bfloat16):
    values = scale * jax.random.normal(rng, shape, jnp.float32)
    if shards:
        values = values * steps_of(rng, shape, shards, -0.22, 0.18)
    return jnp.clip(strengthened(values, jax.random.fold_in(rng, 3), *heavy), -reach, reach).astype(kind)


def setup_inputs(seed: int = 0) -> dict:
    key_list = jax.random.split(jax.random.key(seed), 16)
    attn_grad = gaussian_with(key_list[0], (N_REP, LAYERS, 4, D, D), 1.0, 16.0, ((0, 8), (3, 64)), (3, 4, 64, 4.0))
    attn_error = gaussian(key_list[1], (N_REP, LAYERS, 4, D, D), 1.0, 6.0, ((0, 8), (3, 64)), jnp.float32)
    attn_basis = gaussian(key_list[2], (LAYERS, 4, D, RANK), D ** -0.5, 0.21875, ((2, 64),), jnp.float32)
    attn_roots = draw_attn_roots(jax.random.fold_in(key_list[15], 71), 0)
    attn_momentum = gaussian(key_list[4], (LAYERS, 4, D, D), 0.5, 4.0, ((2, 64),), jnp.float32)
    attn_weights = gaussian(key_list[5], (LAYERS, 4, D, D), D ** -0.5, 0.21875, ((2, 64),), jnp.float32)
    mlp_grad = gaussian_with(key_list[6], (N_REP, LAYERS, 2, D, FF), 1.0, 16.0, ((0, 8), (3, 64)), (3, 4, 64, 4.0))
    mlp_error = gaussian(key_list[7], (N_REP, LAYERS, 2, D, FF), 1.0, 6.0, ((0, 8), (3, 64)), jnp.float32)
    mlp_basis = gaussian(key_list[8], (LAYERS, 2, FF, RANK), FF ** -0.5, 0.109375, ((2, 64),), jnp.float32)
    mlp_roots = draw_mlp_roots(jax.random.fold_in(key_list[15], 71), 0)
    mlp_momentum = gaussian(key_list[10], (LAYERS, 2, D, FF), 0.5, 4.0, ((2, 64),), jnp.float32)
    mlp_weights = gaussian(key_list[11], (LAYERS, 2, D, FF), D ** -0.5, 0.21875, ((2, 64),), jnp.float32)
    small_grad = gaussian(key_list[12], (N_REP, LAYERS, VEC), 1.0, 6.0, ((0, 8), (2, 64)))
    small_momentum = gaussian(key_list[13], (LAYERS, VEC), 0.5, 4.0, ((1, 64),), jnp.float32)
    small_weights = gaussian(key_list[14], (LAYERS, VEC), 1.0, 6.0, ((1, 64),), jnp.float32)
    return {"attn_grad": attn_grad, "attn_error": attn_error, "attn_basis": attn_basis, "attn_roots": attn_roots, "attn_momentum": attn_momentum, "attn_weights": attn_weights, "mlp_grad": mlp_grad, "mlp_error": mlp_error, "mlp_basis": mlp_basis, "mlp_roots": mlp_roots, "mlp_momentum": mlp_momentum, "mlp_weights": mlp_weights, "small_grad": small_grad, "small_momentum": small_momentum, "small_weights": small_weights}


momentum_decay = 0.9
learn_rate = 0.05


def group_step(gradient, error, basis, inverse_roots, momentum, weights):
    highest = lax.Precision.HIGHEST
    merged = gradient.astype(jnp.float32) + error

    def rows_product(factor):
        return jnp.einsum("ilkrc,lkcn->lkrn", merged, factor, precision=highest)

    def cols_product(factor):
        return jnp.einsum("ilkrc,lkrn->lkcn", merged, factor, precision=highest)

    def rotate(factor, round_index):
        return jnp.einsum("lkrn,lknm->lkrm", factor, inverse_roots[:, :, round_index], precision=highest)

    left_hat = rotate(rows_product(basis), 0)
    right_hat = rotate(cols_product(left_hat), 1)
    left_factor = rotate(rows_product(right_hat), 2)
    right_factor = cols_product(left_factor) / float(N_REP)
    approx = jnp.einsum("lkrn,lkcn->lkrc", left_factor, right_factor, precision=highest)
    error_out = merged - approx[None]
    momentum_out = momentum_decay * momentum + approx
    weights_out = weights - learn_rate * momentum_out
    return error_out, left_factor, right_factor, momentum_out, weights_out


def reference(attn_grad, attn_error, attn_basis, attn_roots, attn_momentum, attn_weights, mlp_grad, mlp_error, mlp_basis, mlp_roots, mlp_momentum, mlp_weights, small_grad, small_momentum, small_weights):
    attn_parts = group_step(attn_grad, attn_error, attn_basis, attn_roots, attn_momentum, attn_weights)
    mlp_parts = group_step(mlp_grad, mlp_error, mlp_basis, mlp_roots, mlp_momentum, mlp_weights)
    small_mean = jnp.sum(small_grad.astype(jnp.float32), axis=0) / float(N_REP)
    small_momentum_out = momentum_decay * small_momentum + small_mean
    small_weights_out = small_weights - learn_rate * small_momentum_out
    return (attn_parts[0], mlp_parts[0], attn_parts[1], attn_parts[2], mlp_parts[1], mlp_parts[2], attn_parts[3], attn_parts[4], mlp_parts[3], mlp_parts[4], small_momentum_out, small_weights_out)
```

```python
import jax
import jax.numpy as jnp
from jax import lax
from jax.experimental import pallas as pl
from jax.experimental.pallas import tpu as pltpu
from jax.sharding import PartitionSpec as P

momentum_decay = 0.9
learn_rate = 0.05

MESH = pl.DeviceIdType.MESH
HI = lax.Precision.HIGHEST
LANES = 128
TILE = 8


def dot_nn(a, b):
    return lax.dot_general(
        a, b, (((1,), (0,)), ((), ())), precision=HI, preferred_element_type=jnp.float32
    )


def dot_nt(a, b):
    return lax.dot_general(
        a, b, (((1,), (1,)), ((), ())), precision=HI, preferred_element_type=jnp.float32
    )


def dot_tn(a, b):
    return lax.dot_general(
        a, b, (((0,), (0,)), ((), ())), precision=HI, preferred_element_type=jnp.float32
    )


def power_kernel(
    shape,
    x_ref,
    ba_ref,
    bm_ref,
    sg_ref,
    roots_ref,
    y_ref,
    small_ref,
    land_x,
    s_ref,
    land_ba,
    land_bm,
    basis_a,
    basis_m,
    land_sm,
    swap_out,
    swap_in,
    part,
    land_p,
    land_e,
    full,
    x_send,
    x_recv,
    sm_send,
    sm_recv,
    ba_send,
    ba_recv,
    bm_send,
    bm_recv,
    swap_send,
    swap_recv,
    p_send,
    p_recv,
    e_recv,
    g_send,
    ge_send,
    g_recv,
    y_send,
    y_recv,
):
    shards, reps, rows, cols_a, cols_m, rank, tiles = shape
    extra = tiles - shards
    half = shards // 2
    me = lax.axis_index("shard")
    rep = lax.axis_index("rep")
    side = lax.rem(rep, 2)
    pair = rep + 1 - 2 * side
    side_lo = side * half
    mine_in_side = jnp.logical_and(me >= side_lo, me < side_lo + half)

    def peer(step):
        return lax.rem(me + step, shards)

    def rep_peer(step):
        return lax.rem(rep + step, reps)

    def remote(src, dst, send, recv, where):
        return pltpu.make_async_remote_copy(
            src_ref=src,
            dst_ref=dst,
            send_sem=send,
            recv_sem=recv,
            device_id=where,
            device_id_type=MESH,
        )

    barrier = pltpu.get_barrier_semaphore()

    @pl.loop(1, reps)
    def _(step):
        pl.semaphore_signal(
            barrier, inc=1, device_id={"rep": rep_peer(step)}, device_id_type=MESH
        )

    @pl.loop(1, shards)
    def _(step):
        pl.semaphore_signal(barrier, inc=1, device_id={"shard": peer(step)}, device_id_type=MESH)

    pl.semaphore_wait(barrier, reps - 1 + shards - 1)

    def x_copy(step):
        to = rep_peer(step)
        return remote(
            x_ref.at[to], land_x.at[step], x_send.at[step], x_recv.at[step], {"rep": to}
        )

    def small_copy(step, slot):
        return remote(
            sg_ref, land_sm.at[slot], sm_send.at[step], sm_recv.at[slot], {"rep": rep_peer(step)}
        )

    def ba_copy(step, slot):
        return remote(
            ba_ref, land_ba.at[slot], ba_send.at[step], ba_recv.at[slot], {"shard": peer(step)}
        )

    def bm_copy(step, slot):
        return remote(
            bm_ref, land_bm.at[slot], bm_send.at[step], bm_recv.at[slot], {"shard": peer(step)}
        )

    @pl.loop(1, reps)
    def _(step):
        x_copy(step).start()

    @pl.loop(1, shards)
    def _(step):
        ba_copy(step, me).start()

    @pl.when(mine_in_side)
    def _():
        @pl.loop(1, shards)
        def _(step):
            bm_copy(step, me - side_lo).start()

        land_bm[me - side_lo] = bm_ref[...]

    @pl.loop(1, reps)
    def _(step):
        small_copy(step, rep).start()

    land_sm[rep] = sg_ref[...]
    land_ba[me] = ba_ref[...]

    @pl.loop(1, shards)
    def _(step):
        ba_copy(step, peer(step)).wait_recv()

    @pl.loop(0, half)
    def _(slot):
        @pl.when(slot + side_lo != me)
        def _():
            bm_copy(1, slot).wait_recv()

    @pl.loop(0, half)
    def _(slot):
        for core in range(2):
            basis_a[slot, core * rows : (core + 1) * rows, :] = land_ba[2 * slot + core]
        packed = land_bm[slot]
        for group in range(4):
            basis_m[slot, group * rows : (group + 1) * rows, :] = packed[
                :, group * rank : (group + 1) * rank
            ]

    s_ref[...] = jnp.zeros_like(s_ref)
    s_ref[0:rows, :] = x_ref[rep]

    @pl.loop(1, reps)
    def _(step):
        x_copy(step).wait_recv()
        s_ref[0:rows, :] += land_x[step]

    def swapped(turn, term):
        swap_out[turn] = term
        copy = remote(
            swap_out.at[turn],
            swap_in.at[turn],
            swap_send.at[turn],
            swap_recv.at[turn],
            {"rep": pair},
        )
        copy.start()
        copy.wait()
        return term + swap_in[turn]

    def right_round(turn, left_a, left_m, scale):
        mine = part.at[turn]
        right_a = dot_tn(left_a, s_ref[:, 0:cols_a])
        right_m = dot_tn(left_m, s_ref[:, cols_a : cols_a + cols_m])
        blocks_a = cols_a // LANES
        deep = rank // TILE
        for block in range((cols_a + cols_m) // LANES):
            if block < blocks_a:
                value = right_a[:, block * LANES : (block + 1) * LANES]
            else:
                at = block - blocks_a
                value = right_m[:, at * LANES : (at + 1) * LANES]
            part[turn, block * deep : (block + 1) * deep] = value.reshape(deep, TILE, LANES)

        def p_copy(step, slot):
            to = peer(step)
            return remote(
                mine.at[to],
                land_p.at[turn, slot],
                p_send.at[step],
                p_recv.at[turn, slot],
                {"shard": to},
            )

        def e_copy(owner, slot):
            return remote(
                mine.at[shards + owner],
                land_e.at[turn, slot],
                p_send.at[shards + owner],
                e_recv.at[turn, slot],
                {"shard": owner},
            )

        @pl.loop(0, extra)
        def _(owner):
            @pl.when(owner != me)
            def _():
                e_copy(owner, me).start()

        @pl.loop(1, shards)
        def _(step):
            p_copy(step, me).start()

        def g_copy(step, slot):
            return remote(
                full.at[turn, slot],
                full.at[turn, slot],
                g_send.at[step],
                g_recv.at[turn, slot],
                {"shard": peer(step)},
            )

        def ge_copy(step, slot):
            return remote(
                full.at[turn, shards + slot],
                full.at[turn, shards + slot],
                ge_send.at[step],
                g_recv.at[turn, shards + slot],
                {"shard": peer(step)},
            )

        @pl.when(me < extra)
        def _():
            land_e[turn, me] = part[turn, shards + me]

            @pl.loop(1, shards)
            def _(step):
                e_copy(0, peer(step)).wait_recv()

            full[turn, shards + me] = jnp.sum(land_e[turn], axis=0) * scale

            @pl.loop(1, shards)
            def _(step):
                ge_copy(step, me).start()

        land_p[turn, me] = part[turn, me]

        @pl.loop(1, shards)
        def _(step):
            p_copy(step, peer(step)).wait_recv()

        full[turn, me] = jnp.sum(land_p[turn], axis=0) * scale

        @pl.loop(1, shards)
        def _(step):
            g_copy(step, me).start()

        @pl.loop(0, extra)
        def _(owner):
            @pl.when(owner != me)
            def _():
                ge_copy(1, owner).wait_recv()

        @pl.loop(1, shards)
        def _(step):
            g_copy(step, peer(step)).wait_recv()

        @pl.loop(1, shards)
        def _(step):
            p_copy(step, me).wait_send()
            g_copy(step, me).wait_send()

        @pl.loop(0, extra)
        def _(owner):
            @pl.when(owner != me)
            def _():
                e_copy(owner, me).wait_send()

        @pl.when(me < extra)
        def _():
            @pl.loop(1, shards)
            def _(step):
                ge_copy(step, me).wait_send()

        pieces = [
            full[turn, block * deep : (block + 1) * deep].reshape(rank, LANES)
            for block in range((cols_a + cols_m) // LANES)
        ]
        return (
            jnp.concatenate(pieces[:blocks_a], axis=1),
            jnp.concatenate(pieces[blocks_a:], axis=1),
        )

    basis_full_a = basis_a[...].reshape(cols_a, rank)
    basis_full_m = basis_m[...].reshape(cols_m, rank)
    first_m = dot_nn(s_ref[:, cols_a : cols_a + cols_m], basis_full_m)
    first_a = dot_nn(s_ref[:, 0:cols_a], basis_full_a)
    first_m = swapped(0, first_m)
    lhat_a = dot_nn(first_a, roots_ref[0, 0])
    lhat_m = dot_nn(first_m, roots_ref[1, 0])
    one_a, one_m = right_round(0, lhat_a, lhat_m, 1.0)
    second_m = swapped(1, dot_nt(s_ref[:, cols_a : cols_a + cols_m], one_m))
    second_a = dot_nt(s_ref[:, 0:cols_a], one_a)
    left_a = dot_nn(dot_nn(second_a, roots_ref[0, 1]), roots_ref[0, 2])
    left_m = dot_nn(dot_nn(second_m, roots_ref[1, 1]), roots_ref[1, 2])
    right_a, right_m = right_round(1, left_a, left_m, 1.0 / reps)

    y_ref[rep, :, 0:cols_a] = dot_nn(left_a, right_a)[0:rows]
    y_ref[rep, :, cols_a : cols_a + cols_m] = dot_nn(left_m, right_m)[0:rows]
    padded = left_a.shape[0]
    line = lax.broadcasted_iota(jnp.int32, (padded, cols_a), 0)
    column = lax.broadcasted_iota(jnp.int32, (padded, cols_a), 1)
    pick_a = jnp.where(column == me * rows + line, 1.0, 0.0).astype(jnp.float32)
    line = lax.broadcasted_iota(jnp.int32, (padded, cols_m), 0)
    column = lax.broadcasted_iota(jnp.int32, (padded, cols_m), 1)
    factors = [left_a, left_m, dot_nt(pick_a, right_a)]
    for group in range(4):
        start = (me - side_lo) * (4 * rows) + group * rows
        pick_m = jnp.where(column == start + line, 1.0, 0.0).astype(jnp.float32)
        factors.append(dot_nt(pick_m, right_m))
    factors.append(jnp.zeros_like(left_a))
    for at, factor in enumerate(factors):
        lo = cols_a + cols_m + at * rank
        y_ref[rep, :, lo : lo + rank] = factor[0:rows]

    def y_copy(step, slot):
        return remote(
            y_ref.at[slot], y_ref.at[slot], y_send.at[step], y_recv.at[slot], {"rep": rep_peer(step)}
        )

    @pl.loop(1, reps)
    def _(step):
        y_copy(step, rep).start()

    @pl.loop(1, reps)
    def _(step):
        small_copy(step, rep_peer(step)).wait_recv()

    total = land_sm[0]
    for slot in range(1, reps):
        total = total + land_sm[slot]
    small_ref[...] = total

    @pl.loop(1, shards)
    def _(step):
        ba_copy(step, me).wait_send()

    @pl.when(mine_in_side)
    def _():
        @pl.loop(1, shards)
        def _(step):
            bm_copy(step, me - side_lo).wait_send()

    @pl.loop(1, reps)
    def _(step):
        x_copy(step).wait_send()
        small_copy(step, rep).wait_send()

    @pl.loop(1, reps)
    def _(step):
        y_copy(step, rep_peer(step)).wait_recv()
        y_copy(step, rep).wait_send()


def power_call(shape, x, ba, bm, sg, roots):
    shards, reps, rows, cols_a, cols_m, rank, tiles = shape
    padded = 16
    half = shards // 2
    width = cols_a + cols_m
    wide = width + 8 * rank
    f32 = jnp.float32
    vmem = pl.BlockSpec(memory_space=pltpu.VMEM)
    dma = pltpu.SemaphoreType.DMA

    def body(*refs):
        power_kernel(shape, *refs)

    return pl.pallas_call(
        body,
        out_shape=(
            jax.ShapeDtypeStruct((reps, rows, wide), f32),
            jax.ShapeDtypeStruct(sg.shape, f32),
        ),
        in_specs=[vmem] * 5,
        out_specs=(vmem, vmem),
        scratch_shapes=[
            pltpu.VMEM((reps, rows, width), f32),
            pltpu.VMEM((padded, width), f32),
            pltpu.VMEM((shards, rows, rank), f32),
            pltpu.VMEM((half, rows, 4 * rank), f32),
            pltpu.VMEM((half, 2 * rows, rank), f32),
            pltpu.VMEM((half, 4 * rows, rank), f32),
            pltpu.VMEM((reps,) + sg.shape, f32),
            pltpu.VMEM((2, padded, rank), f32),
            pltpu.VMEM((2, padded, rank), f32),
            pltpu.VMEM((2, tiles, TILE, LANES), f32),
            pltpu.VMEM((2, shards, TILE, LANES), f32),
            pltpu.VMEM((2, shards, TILE, LANES), f32),
            pltpu.VMEM((2, tiles, TILE, LANES), f32),
            dma((reps,)),
            dma((reps,)),
            dma((reps,)),
            dma((reps,)),
            dma((shards,)),
            dma((shards,)),
            dma((shards,)),
            dma((half,)),
            dma((2,)),
            dma((2,)),
            dma((tiles,)),
            dma((2, shards)),
            dma((2, shards)),
            dma((shards,)),
            dma((shards,)),
            dma((2, tiles)),
            dma((reps,)),
            dma((reps,)),
        ],
        compiler_params=pltpu.CompilerParams(collective_id=0, has_side_effects=True),
        name="power_rounds",
    )(x, ba, bm, sg, roots)


def update(merged, approx, momentum, weights):
    error_out = (merged - approx)[None]
    momentum_out = momentum_decay * momentum + approx
    weights_out = weights - learn_rate * momentum_out
    return (error_out, momentum_out, weights_out)


def pick(array, index):
    return lax.dynamic_index_in_dim(array, index, 0, keepdims=False)


def per_device(
    attn_grad,
    attn_error,
    attn_basis,
    attn_roots,
    attn_momentum,
    attn_weights,
    mlp_grad,
    mlp_error,
    mlp_basis,
    mlp_roots,
    mlp_momentum,
    mlp_weights,
    small_grad,
    small_momentum,
    small_weights,
):
    shards, reps = lax.axis_size("shard"), lax.axis_size("rep")
    layers, kinds_a, rows, cols_a = attn_error.shape[1:]
    kinds_m, _, columns_m = mlp_error.shape[2:]
    rank = attn_basis.shape[-1]
    mats_a, mats_m = layers * kinds_a, layers * kinds_m
    cols_m = columns_m // 2
    assert mats_a == reps and 2 * mats_m == reps
    rep = lax.axis_index("rep")

    attn_merged = attn_grad[0].astype(jnp.float32) + attn_error[0]
    mlp_merged = mlp_grad[0].astype(jnp.float32) + mlp_error[0]
    x = jnp.concatenate(
        [
            attn_merged.reshape(mats_a, rows, cols_a),
            mlp_merged.reshape(mats_m, rows, 2, cols_m)
            .transpose(0, 2, 1, 3)
            .reshape(reps, rows, cols_m),
        ],
        axis=2,
    )
    ba = pick(attn_basis.reshape(mats_a, rows, rank), rep)
    bm = pick(mlp_basis.reshape(mats_m, 4, rows, rank), rep // 2)
    bm = bm.transpose(1, 0, 2).reshape(rows, 4 * rank)
    roots = jnp.stack(
        [
            pick(attn_roots.reshape(mats_a, 3, rank, rank), rep),
            pick(mlp_roots.reshape(mats_m, 3, rank, rank), rep // 2),
        ]
    )
    entries = small_grad.shape[1] * small_grad.shape[2]
    lines = -(-entries // LANES)
    sg = small_grad[0].astype(jnp.float32).reshape(entries)
    sg = jnp.pad(sg, (0, lines * LANES - entries)).reshape(lines, LANES)
    tiles = (cols_a + cols_m) * rank // (TILE * LANES)

    y, small = power_call((shards, reps, rows, cols_a, cols_m, rank, tiles), x, ba, bm, sg, roots)

    attn_approx = y[:, :, :cols_a].reshape(layers, kinds_a, rows, cols_a)
    mlp_approx = (
        y[:, :, cols_a : cols_a + cols_m]
        .reshape(mats_m, 2, rows, cols_m)
        .transpose(0, 2, 1, 3)
        .reshape(layers, kinds_m, rows, columns_m)
    )
    factors = y[:, :, cols_a + cols_m :].reshape(reps, rows, 8, rank)
    attn_left = factors[:, :, 0].reshape(layers, kinds_a, rows, rank)
    mlp_left = factors[0::2, :, 1].reshape(layers, kinds_m, rows, rank)
    attn_right = factors[:, :, 2].reshape(layers, kinds_a, rows, rank)
    mlp_right = factors[0::2, :, 3:7] + factors[1::2, :, 3:7]
    mlp_right = mlp_right.transpose(0, 2, 1, 3).reshape(layers, kinds_m, 4 * rows, rank)

    attn_error_out, attn_momentum_out, attn_weights_out = update(
        attn_merged, attn_approx, attn_momentum, attn_weights
    )
    mlp_error_out, mlp_momentum_out, mlp_weights_out = update(
        mlp_merged, mlp_approx, mlp_momentum, mlp_weights
    )
    small_total = small.reshape(lines * LANES)[:entries].reshape(small_momentum.shape)
    small_mean = small_total / float(reps)
    small_momentum_out = momentum_decay * small_momentum + small_mean
    small_weights_out = small_weights - learn_rate * small_momentum_out
    return (
        attn_error_out,
        mlp_error_out,
        attn_left,
        attn_right,
        mlp_left,
        mlp_right,
        attn_momentum_out,
        attn_weights_out,
        mlp_momentum_out,
        mlp_weights_out,
        small_momentum_out,
        small_weights_out,
    )


def solution(mesh):
    in_specs = (
        P("rep", None, None, "shard", None),
        P("rep", None, None, "shard", None),
        P(None, None, "shard", None),
        P(),
        P(None, None, "shard", None),
        P(None, None, "shard", None),
        P("rep", None, None, "shard", None),
        P("rep", None, None, "shard", None),
        P(None, None, "shard", None),
        P(),
        P(None, None, "shard", None),
        P(None, None, "shard", None),
        P("rep", None, "shard"),
        P(None, "shard"),
        P(None, "shard"),
    )
    out_specs = (
        P("rep", None, None, "shard", None),
        P("rep", None, None, "shard", None),
        P(None, None, "shard", None),
        P(None, None, "shard", None),
        P(None, None, "shard", None),
        P(None, None, "shard", None),
        P(None, None, "shard", None),
        P(None, None, "shard", None),
        P(None, None, "shard", None),
        P(None, None, "shard", None),
        P(None, "shard"),
        P(None, "shard"),
    )
    return jax.shard_map(
        per_device, mesh=mesh, in_specs=in_specs, out_specs=out_specs, check_vma=False
    )
```

```python
import jax
import jax.numpy as jnp
from jax import lax
from jax.experimental import pallas as pl
from jax.experimental.pallas import tpu as pltpu
from jax.sharding import PartitionSpec as P

momentum_decay = 0.9
learn_rate = 0.05

MESH = pl.DeviceIdType.MESH
HI = lax.Precision.HIGHEST
LANES = 128
TILE = 8


def dot_nn(a, b):
    return lax.dot_general(
        a, b, (((1,), (0,)), ((), ())), precision=HI, preferred_element_type=jnp.float32
    )


def dot_nt(a, b):
    return lax.dot_general(
        a, b, (((1,), (1,)), ((), ())), precision=HI, preferred_element_type=jnp.float32
    )


def dot_tn(a, b):
    return lax.dot_general(
        a, b, (((0,), (0,)), ((), ())), precision=HI, preferred_element_type=jnp.float32
    )


GROUP = 8
PIECES = 3


def power_kernel(
    shape,
    x_ref,
    ba_ref,
    bm_ref,
    sg_ref,
    roots_ref,
    y_ref,
    small_ref,
    land_x,
    sum_x,
    s_ref,
    land_ba,
    land_bm,
    basis_a,
    basis_m,
    land_sm,
    swap_out,
    swap_in,
    part,
    land_p,
    part_z,
    land_z,
    full,
    x_send,
    x_recv,
    y_send,
    y_recv,
    sm_send,
    sm_recv,
    b_send,
    b_recv,
    c_send,
    c_recv,
    swap_send,
    swap_recv,
    p_send,
    p_recv,
    z_send,
    z_recv,
    g_send,
    g_recv,
):
    shards, reps, rows, cols_a, cols_m, rank, tiles = shape
    width = cols_a + cols_m
    wide = y_ref.shape[2]
    me = lax.axis_index("shard")
    rep = lax.axis_index("rep")
    side = lax.rem(rep, 2)
    pair = rep + 1 - 2 * side
    core = lax.rem(me, 2)
    deep = lax.rem(me // 2, GROUP)
    flat = (me // (2 * GROUP)) * 2 + core
    way = 1 - 2 * core
    in_side = flat // 4 == side
    near = flat - 4 * side

    def flat_peer(step):
        to = lax.rem(flat + step, GROUP)
        return to, {"shard": (to // 2) * (2 * GROUP) + deep * 2 + lax.rem(to, 2)}

    def deep_peer(step):
        to = lax.rem(deep + step, GROUP)
        return to, {"shard": (flat // 2) * (2 * GROUP) + to * 2 + core}

    def rep_at(offset):
        return lax.rem(rep + offset + 2 * reps, reps)

    def remote(src, dst, send, recv, where):
        return pltpu.make_async_remote_copy(
            src_ref=src,
            dst_ref=dst,
            send_sem=send,
            recv_sem=recv,
            device_id=where,
            device_id_type=MESH,
        )

    barrier = pltpu.get_barrier_semaphore()

    def greet(where):
        pl.semaphore_signal(barrier, inc=1, device_id=where, device_id_type=MESH)

    @pl.loop(1, reps)
    def _(step):
        greet({"rep": rep_at(step)})

    @pl.loop(1, GROUP)
    def _(step):
        greet(flat_peer(step)[1])
        greet(deep_peer(step)[1])

    pl.semaphore_wait(barrier, reps - 1 + 2 * (GROUP - 1))

    def cuts(total):
        count = total // LANES
        share = -(-count // PIECES)
        edges = [min(at * share, count) * LANES for at in range(PIECES + 1)]
        return [slice(lo, hi) for lo, hi in zip(edges[:-1], edges[1:])]

    turns = ((0, 4), (1, 3))

    def x_copy(route, step, piece):
        steps = turns[route][1]
        sign = way if route == 0 else -way
        cut = cuts(width)[piece]
        slot = 4 * route + step
        if step == 0:
            source = x_ref.at[rep_at(steps * sign), :, cut]
        else:
            source = sum_x.at[slot, :, cut]
        return remote(
            source,
            land_x.at[slot, :, cut],
            x_send.at[slot, piece],
            x_recv.at[slot, piece],
            {"rep": rep_at(sign)},
        )

    for piece in range(PIECES):
        for route, _ in turns:
            x_copy(route, 0, piece).start()

    def ba_first(step, slot):
        to, where = flat_peer(step)
        return remote(
            ba_ref, land_ba.at[deep, slot], b_send.at[0, step], b_recv.at[0, slot], where
        )

    def bm_first(step, slot):
        to, where = flat_peer(step)
        return remote(
            bm_ref, land_bm.at[deep, slot], b_send.at[1, step], b_recv.at[1, slot], where
        )

    def ba_second(step, slot):
        to, where = deep_peer(step)
        return remote(
            land_ba.at[slot], land_ba.at[slot], c_send.at[0, step], c_recv.at[0, slot], where
        )

    def bm_second(step, slot):
        to, where = deep_peer(step)
        return remote(
            land_bm.at[slot], land_bm.at[slot], c_send.at[1, step], c_recv.at[1, slot], where
        )

    def small_copy(step, slot):
        return remote(
            sg_ref, land_sm.at[slot], sm_send.at[step], sm_recv.at[slot], {"rep": rep_at(step)}
        )

    @pl.loop(1, GROUP)
    def _(step):
        ba_first(step, flat).start()

    land_ba[deep, flat] = ba_ref[...]

    @pl.when(in_side)
    def _():
        @pl.loop(1, GROUP)
        def _(step):
            bm_first(step, near).start()

        land_bm[deep, near] = bm_ref[...]

    @pl.loop(1, reps)
    def _(step):
        small_copy(step, rep).start()

    land_sm[rep] = sg_ref[...]

    @pl.loop(1, GROUP)
    def _(step):
        ba_first(step, flat_peer(step)[0]).wait_recv()

    @pl.loop(0, 4)
    def _(slot):
        @pl.when(slot != near)
        def _():
            bm_first(1, slot).wait_recv()

    @pl.loop(1, GROUP)
    def _(step):
        ba_second(step, deep).start()
        bm_second(step, deep).start()

    for step in range(1, 4):
        for piece in range(PIECES):
            for route, steps in turns:
                if step < steps:
                    sign = way if route == 0 else -way
                    cut = cuts(width)[piece]
                    x_copy(route, step - 1, piece).wait_recv()
                    sum_x[4 * route + step, :, cut] = (
                        land_x[4 * route + step - 1, :, cut]
                        + x_ref[rep_at((steps - step) * sign), :, cut]
                    )
                    x_copy(route, step, piece).start()

    @pl.loop(1, GROUP)
    def _(step):
        ba_second(step, deep_peer(step)[0]).wait_recv()
        bm_second(step, deep_peer(step)[0]).wait_recv()

    @pl.loop(0, GROUP)
    def _(slot):
        for place in range(GROUP):
            lo = (place % 2) * rows
            basis_a[(place // 2) * GROUP + slot, lo : lo + rows, :] = land_ba[slot, place]
        for place in range(4):
            packed = land_bm[slot, place]
            for group in range(4):
                basis_m[
                    ((place // 2) * GROUP + slot) * 2 + place % 2,
                    group * rows : (group + 1) * rows,
                    :,
                ] = packed[:, group * rank : (group + 1) * rank]

    s_ref[...] = jnp.zeros_like(s_ref)
    for piece in range(PIECES):
        cut = cuts(width)[piece]
        for route, steps in turns:
            x_copy(route, steps - 1, piece).wait_recv()
        s_ref[0:rows, cut] = x_ref[rep, :, cut] + (land_x[3, :, cut] + land_x[6, :, cut])

    def swapped(turn, term):
        swap_out[turn] = term
        copy = remote(
            swap_out.at[turn],
            swap_in.at[turn],
            swap_send.at[turn],
            swap_recv.at[turn],
            {"rep": pair},
        )
        copy.start()
        copy.wait()
        return term + swap_in[turn]

    share = tiles // GROUP
    blocks_a, blocks = cols_a // LANES, width // LANES
    high = rank // TILE

    def right_round(turn, left_a, left_m, scale):
        right_a = dot_tn(left_a, s_ref[:, 0:cols_a])
        right_m = dot_tn(left_m, s_ref[:, cols_a:width])
        for block in range(blocks):
            value, at = (right_a, block) if block < blocks_a else (right_m, block - blocks_a)
            for line in range(high):
                tile = block * high + line
                part[turn, tile // share, tile % share] = value[
                    line * TILE : (line + 1) * TILE, at * LANES : (at + 1) * LANES
                ]

        def p_copy(step, slot):
            to, where = flat_peer(step)
            return remote(
                part.at[turn, to],
                land_p.at[turn, slot],
                p_send.at[turn, step],
                p_recv.at[turn, slot],
                where,
            )

        def z_copy(step, slot):
            to, where = deep_peer(step)
            return remote(
                part_z.at[turn],
                land_z.at[turn, slot],
                z_send.at[turn, step],
                z_recv.at[turn, slot],
                where,
            )

        def g_copy(step, slot):
            to, where = flat_peer(step)
            return remote(
                full.at[turn, slot],
                full.at[turn, slot],
                g_send.at[turn, step],
                g_recv.at[turn, slot],
                where,
            )

        @pl.loop(1, GROUP)
        def _(step):
            p_copy(step, flat).start()

        land_p[turn, flat] = part[turn, flat]

        @pl.loop(1, GROUP)
        def _(step):
            p_copy(step, flat_peer(step)[0]).wait_recv()

        part_z[turn] = jnp.sum(land_p[turn], axis=0)

        @pl.loop(1, GROUP)
        def _(step):
            z_copy(step, deep).start()

        land_z[turn, deep] = part_z[turn]

        @pl.loop(1, GROUP)
        def _(step):
            z_copy(step, deep_peer(step)[0]).wait_recv()

        full[turn, flat] = jnp.sum(land_z[turn], axis=0) * scale

        @pl.loop(1, GROUP)
        def _(step):
            g_copy(step, flat).start()

        @pl.loop(1, GROUP)
        def _(step):
            g_copy(step, flat_peer(step)[0]).wait_recv()

        @pl.loop(1, GROUP)
        def _(step):
            p_copy(step, flat).wait_send()
            z_copy(step, deep).wait_send()
            g_copy(step, flat).wait_send()

        whole = full[turn].reshape(tiles, TILE, LANES)
        pieces = [
            whole[block * high : (block + 1) * high].reshape(rank, LANES) for block in range(blocks)
        ]
        return (
            jnp.concatenate(pieces[:blocks_a], axis=1),
            jnp.concatenate(pieces[blocks_a:], axis=1),
        )

    basis_full_a = basis_a[...].reshape(cols_a, rank)
    basis_full_m = basis_m[...].reshape(cols_m, rank)
    first_m = dot_nn(s_ref[:, cols_a:width], basis_full_m)
    first_a = dot_nn(s_ref[:, 0:cols_a], basis_full_a)
    first_m = swapped(0, first_m)
    lhat_a = dot_nn(first_a, roots_ref[0, 0])
    lhat_m = dot_nn(first_m, roots_ref[1, 0])
    one_a, one_m = right_round(0, lhat_a, lhat_m, 1.0)
    second_m = swapped(1, dot_nt(s_ref[:, cols_a:width], one_m))
    second_a = dot_nt(s_ref[:, 0:cols_a], one_a)
    left_a = dot_nn(dot_nn(second_a, roots_ref[0, 1]), roots_ref[0, 2])
    left_m = dot_nn(dot_nn(second_m, roots_ref[1, 1]), roots_ref[1, 2])
    right_a, right_m = right_round(1, left_a, left_m, 1.0 / reps)

    def y_copy(route, step, piece):
        sign = way if route == 0 else -way
        cut = cuts(wide)[piece]
        block = y_ref.at[rep_at(-step * sign), :, cut]
        slot = 4 * route + step
        return remote(
            block, block, y_send.at[slot, piece], y_recv.at[slot, piece], {"rep": rep_at(sign)}
        )

    def y_landed(route, step, piece):
        sign = way if route == 0 else -way
        block = y_ref.at[rep_at(-(step + 1) * sign), :, cuts(wide)[piece]]
        slot = 4 * route + step
        return remote(
            block, block, y_send.at[slot, piece], y_recv.at[slot, piece], {"rep": rep_at(sign)}
        )

    y_ref[rep, :, 0:cols_a] = dot_nn(left_a, right_a)[0:rows]
    y_ref[rep, :, cols_a:width] = dot_nn(left_m, right_m)[0:rows]
    for piece in range(PIECES - 1):
        for route, _ in turns:
            y_copy(route, 0, piece).start()
    padded = left_a.shape[0]
    line = lax.broadcasted_iota(jnp.int32, (padded, cols_a), 0)
    column = lax.broadcasted_iota(jnp.int32, (padded, cols_a), 1)
    pick_a = jnp.where(column == me * rows + line, 1.0, 0.0).astype(jnp.float32)
    line = lax.broadcasted_iota(jnp.int32, (padded, cols_m), 0)
    column = lax.broadcasted_iota(jnp.int32, (padded, cols_m), 1)
    factors = [left_a, left_m, dot_nt(pick_a, right_a)]
    for group in range(4):
        start = (me - side * (shards // 2)) * (4 * rows) + group * rows
        pick_m = jnp.where(column == start + line, 1.0, 0.0).astype(jnp.float32)
        factors.append(dot_nt(pick_m, right_m))
    factors.append(jnp.zeros_like(left_a))
    for at, factor in enumerate(factors):
        lo = width + at * rank
        y_ref[rep, :, lo : lo + rank] = factor[0:rows]
    for route, _ in turns:
        y_copy(route, 0, PIECES - 1).start()

    for step in range(1, 4):
        for piece in range(PIECES):
            for route, steps in turns:
                if step < steps:
                    y_landed(route, step - 1, piece).wait_recv()
                    y_copy(route, step, piece).start()

    @pl.loop(1, reps)
    def _(step):
        small_copy(step, rep_at(step)).wait_recv()

    total = land_sm[0]
    for slot in range(1, reps):
        total = total + land_sm[slot]
    small_ref[...] = total

    @pl.loop(1, GROUP)
    def _(step):
        ba_first(step, flat).wait_send()
        ba_second(step, deep).wait_send()
        bm_second(step, deep).wait_send()

    @pl.when(in_side)
    def _():
        @pl.loop(1, GROUP)
        def _(step):
            bm_first(step, near).wait_send()

    @pl.loop(1, reps)
    def _(step):
        small_copy(step, rep).wait_send()

    for route, steps in turns:
        for piece in range(PIECES):
            y_landed(route, steps - 1, piece).wait_recv()
            for step in range(steps):
                x_copy(route, step, piece).wait_send()
                y_copy(route, step, piece).wait_send()


def power_call(shape, x, ba, bm, sg, roots):
    shards, reps, rows, cols_a, cols_m, rank, tiles = shape
    padded = 16
    width = cols_a + cols_m
    wide = width + 8 * rank
    share = tiles // GROUP
    assert shards == GROUP * GROUP and reps == GROUP and tiles % GROUP == 0
    f32 = jnp.float32
    vmem = pl.BlockSpec(memory_space=pltpu.VMEM)
    dma = pltpu.SemaphoreType.DMA

    def body(*refs):
        power_kernel(shape, *refs)

    return pl.pallas_call(
        body,
        out_shape=(
            jax.ShapeDtypeStruct((reps, rows, wide), f32),
            jax.ShapeDtypeStruct(sg.shape, f32),
        ),
        in_specs=[vmem] * 5,
        out_specs=(vmem, vmem),
        scratch_shapes=[
            pltpu.VMEM((7, rows, width), f32),
            pltpu.VMEM((7, rows, width), f32),
            pltpu.VMEM((padded, width), f32),
            pltpu.VMEM((GROUP, GROUP, rows, rank), f32),
            pltpu.VMEM((GROUP, 4, rows, 4 * rank), f32),
            pltpu.VMEM((shards // 2, 2 * rows, rank), f32),
            pltpu.VMEM((shards // 2, 4 * rows, rank), f32),
            pltpu.VMEM((reps,) + sg.shape, f32),
            pltpu.VMEM((2, padded, rank), f32),
            pltpu.VMEM((2, padded, rank), f32),
            pltpu.VMEM((2, GROUP, share, TILE, LANES), f32),
            pltpu.VMEM((2, GROUP, share, TILE, LANES), f32),
            pltpu.VMEM((2, share, TILE, LANES), f32),
            pltpu.VMEM((2, GROUP, share, TILE, LANES), f32),
            pltpu.VMEM((2, GROUP, share, TILE, LANES), f32),
            dma((7, PIECES)),
            dma((7, PIECES)),
            dma((7, PIECES)),
            dma((7, PIECES)),
            dma((reps,)),
            dma((reps,)),
            dma((2, GROUP)),
            dma((2, GROUP)),
            dma((2, GROUP)),
            dma((2, GROUP)),
            dma((2,)),
            dma((2,)),
            dma((2, GROUP)),
            dma((2, GROUP)),
            dma((2, GROUP)),
            dma((2, GROUP)),
            dma((2, GROUP)),
            dma((2, GROUP)),
        ],
        compiler_params=pltpu.CompilerParams(collective_id=0, has_side_effects=True),
        name="power_rounds",
    )(x, ba, bm, sg, roots)


def update(merged, approx, momentum, weights):
    error_out = (merged - approx)[None]
    momentum_out = momentum_decay * momentum + approx
    weights_out = weights - learn_rate * momentum_out
    return (error_out, momentum_out, weights_out)


def pick(array, index):
    return lax.dynamic_index_in_dim(array, index, 0, keepdims=False)


def per_device(
    attn_grad,
    attn_error,
    attn_basis,
    attn_roots,
    attn_momentum,
    attn_weights,
    mlp_grad,
    mlp_error,
    mlp_basis,
    mlp_roots,
    mlp_momentum,
    mlp_weights,
    small_grad,
    small_momentum,
    small_weights,
):
    shards, reps = lax.axis_size("shard"), lax.axis_size("rep")
    layers, kinds_a, rows, cols_a = attn_error.shape[1:]
    kinds_m, _, columns_m = mlp_error.shape[2:]
    rank = attn_basis.shape[-1]
    mats_a, mats_m = layers * kinds_a, layers * kinds_m
    cols_m = columns_m // 2
    assert mats_a == reps and 2 * mats_m == reps
    rep = lax.axis_index("rep")

    attn_merged = attn_grad[0].astype(jnp.float32) + attn_error[0]
    mlp_merged = mlp_grad[0].astype(jnp.float32) + mlp_error[0]
    x = jnp.concatenate(
        [
            attn_merged.reshape(mats_a, rows, cols_a),
            mlp_merged.reshape(mats_m, rows, 2, cols_m)
            .transpose(0, 2, 1, 3)
            .reshape(reps, rows, cols_m),
        ],
        axis=2,
    )
    ba = pick(attn_basis.reshape(mats_a, rows, rank), rep)
    bm = pick(mlp_basis.reshape(mats_m, 4, rows, rank), rep // 2)
    bm = bm.transpose(1, 0, 2).reshape(rows, 4 * rank)
    roots = jnp.stack(
        [
            pick(attn_roots.reshape(mats_a, 3, rank, rank), rep),
            pick(mlp_roots.reshape(mats_m, 3, rank, rank), rep // 2),
        ]
    )
    entries = small_grad.shape[1] * small_grad.shape[2]
    lines = -(-entries // LANES)
    sg = small_grad[0].astype(jnp.float32).reshape(entries)
    sg = jnp.pad(sg, (0, lines * LANES - entries)).reshape(lines, LANES)
    tiles = (cols_a + cols_m) * rank // (TILE * LANES)

    y, small = power_call((shards, reps, rows, cols_a, cols_m, rank, tiles), x, ba, bm, sg, roots)

    attn_approx = y[:, :, :cols_a].reshape(layers, kinds_a, rows, cols_a)
    mlp_approx = (
        y[:, :, cols_a : cols_a + cols_m]
        .reshape(mats_m, 2, rows, cols_m)
        .transpose(0, 2, 1, 3)
        .reshape(layers, kinds_m, rows, columns_m)
    )
    factors = y[:, :, cols_a + cols_m :].reshape(reps, rows, 8, rank)
    attn_left = factors[:, :, 0].reshape(layers, kinds_a, rows, rank)
    mlp_left = factors[0::2, :, 1].reshape(layers, kinds_m, rows, rank)
    attn_right = factors[:, :, 2].reshape(layers, kinds_a, rows, rank)
    mlp_right = factors[0::2, :, 3:7] + factors[1::2, :, 3:7]
    mlp_right = mlp_right.transpose(0, 2, 1, 3).reshape(layers, kinds_m, 4 * rows, rank)

    attn_error_out, attn_momentum_out, attn_weights_out = update(
        attn_merged, attn_approx, attn_momentum, attn_weights
    )
    mlp_error_out, mlp_momentum_out, mlp_weights_out = update(
        mlp_merged, mlp_approx, mlp_momentum, mlp_weights
    )
    small_total = small.reshape(lines * LANES)[:entries].reshape(small_momentum.shape)
    small_mean = small_total / float(reps)
    small_momentum_out = momentum_decay * small_momentum + small_mean
    small_weights_out = small_weights - learn_rate * small_momentum_out
    return (
        attn_error_out,
        mlp_error_out,
        attn_left,
        attn_right,
        mlp_left,
        mlp_right,
        attn_momentum_out,
        attn_weights_out,
        mlp_momentum_out,
        mlp_weights_out,
        small_momentum_out,
        small_weights_out,
    )


def solution(mesh):
    in_specs = (
        P("rep", None, None, "shard", None),
        P("rep", None, None, "shard", None),
        P(None, None, "shard", None),
        P(),
        P(None, None, "shard", None),
        P(None, None, "shard", None),
        P("rep", None, None, "shard", None),
        P("rep", None, None, "shard", None),
        P(None, None, "shard", None),
        P(),
        P(None, None, "shard", None),
        P(None, None, "shard", None),
        P("rep", None, "shard"),
        P(None, "shard"),
        P(None, "shard"),
    )
    out_specs = (
        P("rep", None, None, "shard", None),
        P("rep", None, None, "shard", None),
        P(None, None, "shard", None),
        P(None, None, "shard", None),
        P(None, None, "shard", None),
        P(None, None, "shard", None),
        P(None, None, "shard", None),
        P(None, None, "shard", None),
        P(None, None, "shard", None),
        P(None, None, "shard", None),
        P(None, "shard"),
        P(None, "shard"),
    )
    return jax.shard_map(
        per_device, mesh=mesh, in_specs=in_specs, out_specs=out_specs, check_vma=False
    )
```

```python
import jax
import jax.numpy as jnp
from jax import lax
from jax.experimental import pallas as pl
from jax.experimental.pallas import tpu as pltpu
from jax.sharding import PartitionSpec as P

momentum_decay = 0.9
learn_rate = 0.05

MESH = pl.DeviceIdType.MESH
HI = lax.Precision.HIGHEST
LANES = 128
TILE = 8


def dot_nn(a, b):
    return lax.dot_general(
        a, b, (((1,), (0,)), ((), ())), precision=HI, preferred_element_type=jnp.float32
    )


def dot_nt(a, b):
    return lax.dot_general(
        a, b, (((1,), (1,)), ((), ())), precision=HI, preferred_element_type=jnp.float32
    )


def dot_tn(a, b):
    return lax.dot_general(
        a, b, (((0,), (0,)), ((), ())), precision=HI, preferred_element_type=jnp.float32
    )


GROUP = 8
PIECES = 3


def power_kernel(
    shape,
    ag_ref,
    ae_ref,
    mg_ref,
    me_ref,
    ab_ref,
    mb_ref,
    ar_ref,
    mr_ref,
    sgrad_ref,
    y_ref,
    small_ref,
    x_ref,
    ba_ref,
    bm_ref,
    sg_ref,
    land_x,
    sum_x,
    s_ref,
    land_ba,
    land_bm,
    basis_a,
    basis_m,
    land_sm,
    swap_out,
    swap_in,
    part,
    land_p,
    part_z,
    land_z,
    full,
    x_send,
    x_recv,
    y_send,
    y_recv,
    sm_send,
    sm_recv,
    b_send,
    b_recv,
    c_send,
    c_recv,
    swap_send,
    swap_recv,
    p_send,
    p_recv,
    z_send,
    z_recv,
    g_send,
    g_recv,
):
    shards, reps, rows, cols_a, cols_m, rank, tiles = shape
    width = cols_a + cols_m
    wide = y_ref.shape[2]
    me = lax.axis_index("shard")
    rep = lax.axis_index("rep")
    side = lax.rem(rep, 2)
    pair = rep + 1 - 2 * side
    core = lax.rem(me, 2)
    deep = lax.rem(me // 2, GROUP)
    flat = (me // (2 * GROUP)) * 2 + core
    way = 1 - 2 * core
    in_side = flat // 4 == side
    near = flat - 4 * side

    def flat_peer(step):
        to = lax.rem(flat + step, GROUP)
        return to, {"shard": (to // 2) * (2 * GROUP) + deep * 2 + lax.rem(to, 2)}

    def deep_peer(step):
        to = lax.rem(deep + step, GROUP)
        return to, {"shard": (flat // 2) * (2 * GROUP) + to * 2 + core}

    def rep_at(offset):
        return lax.rem(rep + offset + 2 * reps, reps)

    def remote(src, dst, send, recv, where):
        return pltpu.make_async_remote_copy(
            src_ref=src,
            dst_ref=dst,
            send_sem=send,
            recv_sem=recv,
            device_id=where,
            device_id_type=MESH,
        )

    barrier = pltpu.get_barrier_semaphore()

    def greet(where):
        pl.semaphore_signal(barrier, inc=1, device_id=where, device_id_type=MESH)

    @pl.loop(1, reps)
    def _(step):
        greet({"rep": rep_at(step)})

    @pl.loop(1, GROUP)
    def _(step):
        greet(flat_peer(step)[1])
        greet(deep_peer(step)[1])

    layers, kinds_a, kinds_m = ag_ref.shape[0], ag_ref.shape[2], mg_ref.shape[2]
    for layer in range(layers):
        for row in range(rows):
            lo = layer * kinds_a
            value = ag_ref[layer, row].astype(jnp.float32) + ae_ref[layer, row]
            x_ref[lo : lo + kinds_a, row, 0:cols_a] = value
            value = mg_ref[layer, row].astype(jnp.float32) + me_ref[layer, row]
            for kind in range(kinds_m):
                for part_of in range(2):
                    cut = slice(part_of * cols_m, (part_of + 1) * cols_m)
                    at = (layer * kinds_m + kind) * 2 + part_of
                    x_ref[at, row : row + 1, cols_a:width] = value[kind : kind + 1, cut]

    spread = ab_ref[rep // kinds_a]
    chosen = lax.broadcasted_iota(jnp.int32, spread.shape, 1) == lax.rem(rep, kinds_a)
    ba_ref[...] = jnp.sum(jnp.where(chosen, spread, 0.0), axis=1)
    own = rep // 2
    upright = mb_ref[own // kinds_m, lax.rem(own, kinds_m)].T
    for group in range(4):
        bm_ref[:, group * rank : (group + 1) * rank] = upright[group * rows : (group + 1) * rows]
    sg_ref[...] = jnp.zeros_like(sg_ref)
    sg_ref[:, 0 : sgrad_ref.shape[1]] = sgrad_ref[...].astype(jnp.float32)

    pl.semaphore_wait(barrier, reps - 1 + 2 * (GROUP - 1))

    def cuts(total):
        count = total // LANES
        share = -(-count // PIECES)
        edges = [min(at * share, count) * LANES for at in range(PIECES + 1)]
        return [slice(lo, hi) for lo, hi in zip(edges[:-1], edges[1:])]

    turns = ((0, 4), (1, 3))

    def x_copy(route, step, piece):
        steps = turns[route][1]
        sign = way if route == 0 else -way
        cut = cuts(width)[piece]
        slot = 4 * route + step
        if step == 0:
            source = x_ref.at[rep_at(steps * sign), :, cut]
        else:
            source = sum_x.at[slot, :, cut]
        return remote(
            source,
            land_x.at[slot, :, cut],
            x_send.at[slot, piece],
            x_recv.at[slot, piece],
            {"rep": rep_at(sign)},
        )

    for piece in range(PIECES):
        for route, _ in turns:
            x_copy(route, 0, piece).start()

    def ba_first(step, slot):
        to, where = flat_peer(step)
        return remote(
            ba_ref, land_ba.at[deep, slot], b_send.at[0, step], b_recv.at[0, slot], where
        )

    def bm_first(step, slot):
        to, where = flat_peer(step)
        return remote(
            bm_ref, land_bm.at[deep, slot], b_send.at[1, step], b_recv.at[1, slot], where
        )

    def ba_second(step, slot):
        to, where = deep_peer(step)
        return remote(
            land_ba.at[slot], land_ba.at[slot], c_send.at[0, step], c_recv.at[0, slot], where
        )

    def bm_second(step, slot):
        to, where = deep_peer(step)
        return remote(
            land_bm.at[slot], land_bm.at[slot], c_send.at[1, step], c_recv.at[1, slot], where
        )

    def small_copy(step, slot):
        return remote(
            sg_ref, land_sm.at[slot], sm_send.at[step], sm_recv.at[slot], {"rep": rep_at(step)}
        )

    @pl.loop(1, GROUP)
    def _(step):
        ba_first(step, flat).start()

    land_ba[deep, flat] = ba_ref[...]

    @pl.when(in_side)
    def _():
        @pl.loop(1, GROUP)
        def _(step):
            bm_first(step, near).start()

        land_bm[deep, near] = bm_ref[...]

    @pl.loop(1, reps)
    def _(step):
        small_copy(step, rep).start()

    land_sm[rep] = sg_ref[...]

    @pl.loop(1, GROUP)
    def _(step):
        ba_first(step, flat_peer(step)[0]).wait_recv()

    @pl.loop(0, 4)
    def _(slot):
        @pl.when(slot != near)
        def _():
            bm_first(1, slot).wait_recv()

    @pl.loop(1, GROUP)
    def _(step):
        ba_second(step, deep).start()
        bm_second(step, deep).start()

    for step in range(1, 4):
        for piece in range(PIECES):
            for route, steps in turns:
                if step < steps:
                    sign = way if route == 0 else -way
                    cut = cuts(width)[piece]
                    x_copy(route, step - 1, piece).wait_recv()
                    sum_x[4 * route + step, :, cut] = (
                        land_x[4 * route + step - 1, :, cut]
                        + x_ref[rep_at((steps - step) * sign), :, cut]
                    )
                    x_copy(route, step, piece).start()

    @pl.loop(1, GROUP)
    def _(step):
        ba_second(step, deep_peer(step)[0]).wait_recv()
        bm_second(step, deep_peer(step)[0]).wait_recv()

    @pl.loop(0, GROUP)
    def _(slot):
        for place in range(GROUP):
            lo = (place % 2) * rows
            basis_a[(place // 2) * GROUP + slot, lo : lo + rows, :] = land_ba[slot, place]
        for place in range(4):
            packed = land_bm[slot, place]
            for group in range(4):
                basis_m[
                    ((place // 2) * GROUP + slot) * 2 + place % 2,
                    group * rows : (group + 1) * rows,
                    :,
                ] = packed[:, group * rank : (group + 1) * rank]

    s_ref[...] = jnp.zeros_like(s_ref)
    for piece in range(PIECES):
        cut = cuts(width)[piece]
        for route, steps in turns:
            x_copy(route, steps - 1, piece).wait_recv()
        s_ref[0:rows, cut] = x_ref[rep, :, cut] + (land_x[3, :, cut] + land_x[6, :, cut])

    def swapped(turn, term):
        swap_out[turn] = term
        copy = remote(
            swap_out.at[turn],
            swap_in.at[turn],
            swap_send.at[turn],
            swap_recv.at[turn],
            {"rep": pair},
        )
        copy.start()
        copy.wait()
        return term + swap_in[turn]

    share = tiles // GROUP
    blocks_a, blocks = cols_a // LANES, width // LANES
    high = rank // TILE

    def right_round(turn, left_a, left_m, scale):
        right_a = dot_tn(left_a, s_ref[:, 0:cols_a])
        right_m = dot_tn(left_m, s_ref[:, cols_a:width])
        for block in range(blocks):
            value, at = (right_a, block) if block < blocks_a else (right_m, block - blocks_a)
            for line in range(high):
                tile = block * high + line
                part[turn, tile // share, tile % share] = value[
                    line * TILE : (line + 1) * TILE, at * LANES : (at + 1) * LANES
                ]

        def p_copy(step, slot):
            to, where = flat_peer(step)
            return remote(
                part.at[turn, to],
                land_p.at[turn, slot],
                p_send.at[turn, step],
                p_recv.at[turn, slot],
                where,
            )

        def z_copy(step, slot):
            to, where = deep_peer(step)
            return remote(
                part_z.at[turn],
                land_z.at[turn, slot],
                z_send.at[turn, step],
                z_recv.at[turn, slot],
                where,
            )

        def g_copy(step, slot):
            to, where = flat_peer(step)
            return remote(
                full.at[turn, slot],
                full.at[turn, slot],
                g_send.at[turn, step],
                g_recv.at[turn, slot],
                where,
            )

        @pl.loop(1, GROUP)
        def _(step):
            p_copy(step, flat).start()

        land_p[turn, flat] = part[turn, flat]

        @pl.loop(1, GROUP)
        def _(step):
            p_copy(step, flat_peer(step)[0]).wait_recv()

        part_z[turn] = jnp.sum(land_p[turn], axis=0)

        @pl.loop(1, GROUP)
        def _(step):
            z_copy(step, deep).start()

        land_z[turn, deep] = part_z[turn]

        @pl.loop(1, GROUP)
        def _(step):
            z_copy(step, deep_peer(step)[0]).wait_recv()

        full[turn, flat] = jnp.sum(land_z[turn], axis=0) * scale

        @pl.loop(1, GROUP)
        def _(step):
            g_copy(step, flat).start()

        @pl.loop(1, GROUP)
        def _(step):
            g_copy(step, flat_peer(step)[0]).wait_recv()

        @pl.loop(1, GROUP)
        def _(step):
            p_copy(step, flat).wait_send()
            z_copy(step, deep).wait_send()
            g_copy(step, flat).wait_send()

        whole = full[turn].reshape(tiles, TILE, LANES)
        pieces = [
            whole[block * high : (block + 1) * high].reshape(rank, LANES) for block in range(blocks)
        ]
        return (
            jnp.concatenate(pieces[:blocks_a], axis=1),
            jnp.concatenate(pieces[blocks_a:], axis=1),
        )

    basis_full_a = basis_a[...].reshape(cols_a, rank)
    basis_full_m = basis_m[...].reshape(cols_m, rank)
    first_m = dot_nn(s_ref[:, cols_a:width], basis_full_m)
    first_a = dot_nn(s_ref[:, 0:cols_a], basis_full_a)
    first_m = swapped(0, first_m)
    lhat_a = dot_nn(first_a, ar_ref[rep, 0])
    lhat_m = dot_nn(first_m, mr_ref[rep // 2, 0])
    one_a, one_m = right_round(0, lhat_a, lhat_m, 1.0)
    second_m = swapped(1, dot_nt(s_ref[:, cols_a:width], one_m))
    second_a = dot_nt(s_ref[:, 0:cols_a], one_a)
    left_a = dot_nn(dot_nn(second_a, ar_ref[rep, 1]), ar_ref[rep, 2])
    left_m = dot_nn(dot_nn(second_m, mr_ref[rep // 2, 1]), mr_ref[rep // 2, 2])
    right_a, right_m = right_round(1, left_a, left_m, 1.0 / reps)

    def y_copy(route, step, piece):
        sign = way if route == 0 else -way
        cut = cuts(wide)[piece]
        block = y_ref.at[rep_at(-step * sign), :, cut]
        slot = 4 * route + step
        return remote(
            block, block, y_send.at[slot, piece], y_recv.at[slot, piece], {"rep": rep_at(sign)}
        )

    def y_landed(route, step, piece):
        sign = way if route == 0 else -way
        block = y_ref.at[rep_at(-(step + 1) * sign), :, cuts(wide)[piece]]
        slot = 4 * route + step
        return remote(
            block, block, y_send.at[slot, piece], y_recv.at[slot, piece], {"rep": rep_at(sign)}
        )

    y_ref[rep, :, 0:cols_a] = dot_nn(left_a, right_a)[0:rows]
    y_ref[rep, :, cols_a:width] = dot_nn(left_m, right_m)[0:rows]
    for piece in range(PIECES - 1):
        for route, _ in turns:
            y_copy(route, 0, piece).start()
    padded = left_a.shape[0]
    line = lax.broadcasted_iota(jnp.int32, (padded, cols_a), 0)
    column = lax.broadcasted_iota(jnp.int32, (padded, cols_a), 1)
    pick_a = jnp.where(column == me * rows + line, 1.0, 0.0).astype(jnp.float32)
    line = lax.broadcasted_iota(jnp.int32, (padded, cols_m), 0)
    column = lax.broadcasted_iota(jnp.int32, (padded, cols_m), 1)
    factors = [left_a, left_m, dot_nt(pick_a, right_a)]
    for group in range(4):
        start = (me - side * (shards // 2)) * (4 * rows) + group * rows
        pick_m = jnp.where(column == start + line, 1.0, 0.0).astype(jnp.float32)
        factors.append(dot_nt(pick_m, right_m))
    factors.append(jnp.zeros_like(left_a))
    for at, factor in enumerate(factors):
        lo = width + at * rank
        y_ref[rep, :, lo : lo + rank] = factor[0:rows]
    for route, _ in turns:
        y_copy(route, 0, PIECES - 1).start()

    for step in range(1, 4):
        for piece in range(PIECES):
            for route, steps in turns:
                if step < steps:
                    y_landed(route, step - 1, piece).wait_recv()
                    y_copy(route, step, piece).start()

    @pl.loop(1, reps)
    def _(step):
        small_copy(step, rep_at(step)).wait_recv()

    total = land_sm[0]
    for slot in range(1, reps):
        total = total + land_sm[slot]
    small_ref[...] = total

    @pl.loop(1, GROUP)
    def _(step):
        ba_first(step, flat).wait_send()
        ba_second(step, deep).wait_send()
        bm_second(step, deep).wait_send()

    @pl.when(in_side)
    def _():
        @pl.loop(1, GROUP)
        def _(step):
            bm_first(step, near).wait_send()

    @pl.loop(1, reps)
    def _(step):
        small_copy(step, rep).wait_send()

    for route, steps in turns:
        for piece in range(PIECES):
            y_landed(route, steps - 1, piece).wait_recv()
            for step in range(steps):
                x_copy(route, step, piece).wait_send()
                y_copy(route, step, piece).wait_send()


def power_call(shape, *operands):
    shards, reps, rows, cols_a, cols_m, rank, tiles = shape
    padded = 16
    width = cols_a + cols_m
    wide = width + 8 * rank
    share = tiles // GROUP
    assert shards == GROUP * GROUP and reps == GROUP and tiles % GROUP == 0
    f32 = jnp.float32
    vmem = pl.BlockSpec(memory_space=pltpu.VMEM)
    dma = pltpu.SemaphoreType.DMA
    layers, entries = operands[-1].shape
    small = (layers, -(-entries // LANES) * LANES)

    def body(*refs):
        power_kernel(shape, *refs)

    return pl.pallas_call(
        body,
        out_shape=(
            jax.ShapeDtypeStruct((reps, rows, wide), f32),
            jax.ShapeDtypeStruct(small, f32),
        ),
        in_specs=[vmem] * len(operands),
        out_specs=(vmem, vmem),
        scratch_shapes=[
            pltpu.VMEM((reps, rows, width), f32),
            pltpu.VMEM((rows, rank), f32),
            pltpu.VMEM((rows, 4 * rank), f32),
            pltpu.VMEM(small, f32),
            pltpu.VMEM((7, rows, width), f32),
            pltpu.VMEM((7, rows, width), f32),
            pltpu.VMEM((padded, width), f32),
            pltpu.VMEM((GROUP, GROUP, rows, rank), f32),
            pltpu.VMEM((GROUP, 4, rows, 4 * rank), f32),
            pltpu.VMEM((shards // 2, 2 * rows, rank), f32),
            pltpu.VMEM((shards // 2, 4 * rows, rank), f32),
            pltpu.VMEM((reps,) + small, f32),
            pltpu.VMEM((2, padded, rank), f32),
            pltpu.VMEM((2, padded, rank), f32),
            pltpu.VMEM((2, GROUP, share, TILE, LANES), f32),
            pltpu.VMEM((2, GROUP, share, TILE, LANES), f32),
            pltpu.VMEM((2, share, TILE, LANES), f32),
            pltpu.VMEM((2, GROUP, share, TILE, LANES), f32),
            pltpu.VMEM((2, GROUP, share, TILE, LANES), f32),
        ]
        + [dma((7, PIECES))] * 4
        + [dma((reps,))] * 2
        + [dma((2, GROUP))] * 4
        + [dma((2,))] * 2
        + [dma((2, GROUP))] * 6,
        compiler_params=pltpu.CompilerParams(collective_id=0, has_side_effects=True),
        name="power_rounds",
    )(*operands)


def update_kernel(
    shape,
    y_ref,
    small_ref,
    ag_ref,
    ae_ref,
    am_ref,
    aw_ref,
    mg_ref,
    me_ref,
    mm_ref,
    mw_ref,
    sm_ref,
    sw_ref,
    ae_out,
    me_out,
    al_out,
    ar_out,
    ml_out,
    mr_out,
    am_out,
    aw_out,
    mm_out,
    mw_out,
    sm_out,
    sw_out,
    turned,
):
    shards, reps, rows, cols_a, cols_m, rank, tiles = shape
    width = cols_a + cols_m
    layers, kinds_a, kinds_m = ag_ref.shape[0], ag_ref.shape[2], mg_ref.shape[2]

    def finish(grad, error, momentum, weights, approx):
        stepped = momentum_decay * momentum + approx
        return (
            grad.astype(jnp.float32) + error - approx,
            stepped,
            weights - learn_rate * stepped,
        )

    def lanes(at):
        return slice(width + at * rank, width + (at + 1) * rank)

    for layer in range(layers):
        for row in range(rows):
            lo = layer * kinds_a
            approx = y_ref[lo : lo + kinds_a, row, 0:cols_a]
            ae_out[layer, row], am_out[layer, row], aw_out[layer, row] = finish(
                ag_ref[layer, row],
                ae_ref[layer, row],
                am_ref[layer, row],
                aw_ref[layer, row],
                approx,
            )
            al_out[layer, row] = y_ref[lo : lo + kinds_a, row, lanes(0)]
            ar_out[layer, row] = y_ref[lo : lo + kinds_a, row, lanes(2)]
            first = [(layer * kinds_m + kind) * 2 for kind in range(kinds_m)]
            approx = jnp.concatenate(
                [
                    jnp.concatenate(
                        [y_ref[at, row : row + 1, cols_a:width] for at in (one, one + 1)], axis=1
                    )
                    for one in first
                ],
                axis=0,
            )
            me_out[layer, row], mm_out[layer, row], mw_out[layer, row] = finish(
                mg_ref[layer, row],
                me_ref[layer, row],
                mm_ref[layer, row],
                mw_ref[layer, row],
                approx,
            )
            for kind in range(kinds_m):
                ml_out[layer, row, kind : kind + 1] = y_ref[first[kind], row : row + 1, lanes(1)]
        for kind in range(kinds_m):
            one = (layer * kinds_m + kind) * 2
            for group in range(4):
                turned[group * rows : (group + 1) * rows] = (
                    y_ref[one, :, lanes(3 + group)] + y_ref[one + 1, :, lanes(3 + group)]
                )
            mr_out[layer, kind] = turned[...].T
    entries = sm_ref.shape[1]
    mean = small_ref[:, 0:entries] / float(reps)
    stepped = momentum_decay * sm_ref[...] + mean
    sm_out[...] = stepped
    sw_out[...] = sw_ref[...] - learn_rate * stepped


def update_call(shape, *operands):
    shards, reps, rows, cols_a, cols_m, rank, tiles = shape
    f32 = jnp.float32
    attn, mlp, small = operands[3].shape, operands[7].shape, operands[-1].shape
    layers, kinds_a, kinds_m = attn[0], attn[2], mlp[2]
    vmem = pl.BlockSpec(memory_space=pltpu.VMEM)

    def body(*refs):
        update_kernel(shape, *refs)

    shapes = [
        attn,
        mlp,
        (layers, rows, kinds_a, rank),
        (layers, rows, kinds_a, rank),
        (layers, rows, kinds_m, rank),
        (layers, kinds_m, rank, 4 * rows),
        attn,
        attn,
        mlp,
        mlp,
        small,
        small,
    ]
    return pl.pallas_call(
        body,
        out_shape=tuple(jax.ShapeDtypeStruct(each, f32) for each in shapes),
        in_specs=[vmem] * len(operands),
        out_specs=(vmem,) * len(shapes),
        scratch_shapes=[pltpu.VMEM((4 * rows, rank), f32)],
        name="apply_update",
    )(*operands)


def per_device(
    attn_grad,
    attn_error,
    attn_basis,
    attn_roots,
    attn_momentum,
    attn_weights,
    mlp_grad,
    mlp_error,
    mlp_basis,
    mlp_roots,
    mlp_momentum,
    mlp_weights,
    small_grad,
    small_momentum,
    small_weights,
):
    shards, reps = lax.axis_size("shard"), lax.axis_size("rep")
    layers, kinds_a, rows, cols_a = attn_error.shape[1:]
    kinds_m, _, columns_m = mlp_error.shape[2:]
    rank = attn_basis.shape[-1]
    mats_a, mats_m = layers * kinds_a, layers * kinds_m
    cols_m = columns_m // 2
    assert mats_a == reps and 2 * mats_m == reps
    tiles = (cols_a + cols_m) * rank // (TILE * LANES)
    shape = (shards, reps, rows, cols_a, cols_m, rank, tiles)

    def flip(array):
        return array.transpose(0, 2, 1, 3)

    ag, ae = flip(attn_grad[0]), flip(attn_error[0])
    mg, me = flip(mlp_grad[0]), flip(mlp_error[0])
    y, small = power_call(
        shape,
        ag,
        ae,
        mg,
        me,
        flip(attn_basis),
        mlp_basis.transpose(0, 1, 3, 2),
        attn_roots.reshape(mats_a, 3, rank, rank),
        mlp_roots.reshape(mats_m, 3, rank, rank),
        small_grad[0],
    )
    outs = update_call(
        shape,
        y,
        small,
        ag,
        ae,
        flip(attn_momentum),
        flip(attn_weights),
        mg,
        me,
        flip(mlp_momentum),
        flip(mlp_weights),
        small_momentum,
        small_weights,
    )
    return (
        flip(outs[0])[None],
        flip(outs[1])[None],
        flip(outs[2]),
        flip(outs[3]),
        flip(outs[4]),
        outs[5].transpose(0, 1, 3, 2),
        flip(outs[6]),
        flip(outs[7]),
        flip(outs[8]),
        flip(outs[9]),
        outs[10],
        outs[11],
    )


def solution(mesh):
    in_specs = (
        P("rep", None, None, "shard", None),
        P("rep", None, None, "shard", None),
        P(None, None, "shard", None),
        P(),
        P(None, None, "shard", None),
        P(None, None, "shard", None),
        P("rep", None, None, "shard", None),
        P("rep", None, None, "shard", None),
        P(None, None, "shard", None),
        P(),
        P(None, None, "shard", None),
        P(None, None, "shard", None),
        P("rep", None, "shard"),
        P(None, "shard"),
        P(None, "shard"),
    )
    out_specs = (
        P("rep", None, None, "shard", None),
        P("rep", None, None, "shard", None),
        P(None, None, "shard", None),
        P(None, None, "shard", None),
        P(None, None, "shard", None),
        P(None, None, "shard", None),
        P(None, None, "shard", None),
        P(None, None, "shard", None),
        P(None, None, "shard", None),
        P(None, None, "shard", None),
        P(None, "shard"),
        P(None, "shard"),
    )
    return jax.shard_map(
        per_device, mesh=mesh, in_specs=in_specs, out_specs=out_specs, check_vma=False
    )
```

```python
import jax
import jax.numpy as jnp
from jax import lax
from jax.experimental import pallas as pl
from jax.experimental.pallas import tpu as pltpu
from jax.sharding import PartitionSpec as P

momentum_decay = 0.9
learn_rate = 0.05

MESH = pl.DeviceIdType.MESH
HI = lax.Precision.HIGHEST
LANES = 128
TILE = 8


def dot_nn(a, b):
    return lax.dot_general(
        a, b, (((1,), (0,)), ((), ())), precision=HI, preferred_element_type=jnp.float32
    )


def dot_nt(a, b):
    return lax.dot_general(
        a, b, (((1,), (1,)), ((), ())), precision=HI, preferred_element_type=jnp.float32
    )


def dot_tn(a, b):
    return lax.dot_general(
        a, b, (((0,), (0,)), ((), ())), precision=HI, preferred_element_type=jnp.float32
    )


GROUP = 8
PIECES = 3


def power_kernel(
    shape,
    ag_ref,
    ae_ref,
    mg_ref,
    me_ref,
    ab_ref,
    mb_ref,
    ar_ref,
    mr_ref,
    sgrad_ref,
    y_ref,
    small_ref,
    x_ref,
    ba_ref,
    bm_ref,
    sg_ref,
    land_x,
    sum_x,
    s_ref,
    land_ba,
    land_bm,
    basis_a,
    basis_m,
    land_sm,
    swap_out,
    swap_in,
    part,
    land_p,
    part_z,
    land_z,
    full,
    x_send,
    x_recv,
    y_send,
    y_recv,
    sm_send,
    sm_recv,
    b_send,
    b_recv,
    c_send,
    c_recv,
    swap_send,
    swap_recv,
    p_send,
    p_recv,
    z_send,
    z_recv,
    g_send,
    g_recv,
):
    shards, reps, rows, cols_a, cols_m, rank, tiles = shape
    width = cols_a + cols_m
    wide = y_ref.shape[2]
    me = lax.axis_index("shard")
    rep = lax.axis_index("rep")
    side = lax.rem(rep, 2)
    pair = rep + 1 - 2 * side
    core = lax.rem(me, 2)
    deep = lax.rem(me // 2, GROUP)
    flat = (me // (2 * GROUP)) * 2 + core
    way = 1 - 2 * core
    in_side = flat // 4 == side
    near = flat - 4 * side

    def flat_peer(step):
        to = lax.rem(flat + step, GROUP)
        return to, {"shard": (to // 2) * (2 * GROUP) + deep * 2 + lax.rem(to, 2)}

    def deep_peer(step):
        to = lax.rem(deep + step, GROUP)
        return to, {"shard": (flat // 2) * (2 * GROUP) + to * 2 + core}

    def rep_at(offset):
        return lax.rem(rep + offset + 2 * reps, reps)

    def remote(src, dst, send, recv, where):
        return pltpu.make_async_remote_copy(
            src_ref=src,
            dst_ref=dst,
            send_sem=send,
            recv_sem=recv,
            device_id=where,
            device_id_type=MESH,
        )

    barrier = pltpu.get_barrier_semaphore()

    def greet(where):
        pl.semaphore_signal(barrier, inc=1, device_id=where, device_id_type=MESH)

    @pl.loop(1, reps)
    def _(step):
        greet({"rep": rep_at(step)})

    @pl.loop(1, GROUP)
    def _(step):
        greet(flat_peer(step)[1])
        greet(deep_peer(step)[1])

    layers, kinds_a, kinds_m = ag_ref.shape[0], ag_ref.shape[2], mg_ref.shape[2]
    for layer in range(layers):
        for row in range(rows):
            lo = layer * kinds_a
            value = ag_ref[layer, row].astype(jnp.float32) + ae_ref[layer, row]
            x_ref[lo : lo + kinds_a, row, 0:cols_a] = value
            value = mg_ref[layer, row].astype(jnp.float32) + me_ref[layer, row]
            for kind in range(kinds_m):
                for part_of in range(2):
                    cut = slice(part_of * cols_m, (part_of + 1) * cols_m)
                    at = (layer * kinds_m + kind) * 2 + part_of
                    x_ref[at, row : row + 1, cols_a:width] = value[kind : kind + 1, cut]

    spread = ab_ref[rep // kinds_a]
    chosen = lax.broadcasted_iota(jnp.int32, spread.shape, 1) == lax.rem(rep, kinds_a)
    ba_ref[...] = jnp.sum(jnp.where(chosen, spread, 0.0), axis=1)
    own = rep // 2
    upright = mb_ref[own // kinds_m, lax.rem(own, kinds_m)].T
    for group in range(4):
        bm_ref[:, group * rank : (group + 1) * rank] = upright[group * rows : (group + 1) * rows]
    sg_ref[...] = jnp.zeros_like(sg_ref)
    sg_ref[:, 0 : sgrad_ref.shape[1]] = sgrad_ref[...].astype(jnp.float32)

    pl.semaphore_wait(barrier, reps - 1 + 2 * (GROUP - 1))

    def cuts(total):
        count = total // LANES
        share = -(-count // PIECES)
        edges = [min(at * share, count) * LANES for at in range(PIECES + 1)]
        return [slice(lo, hi) for lo, hi in zip(edges[:-1], edges[1:])]

    turns = ((0, 4), (1, 3))

    def x_copy(route, step, piece):
        steps = turns[route][1]
        sign = way if route == 0 else -way
        cut = cuts(width)[piece]
        slot = 4 * route + step
        if step == 0:
            source = x_ref.at[rep_at(steps * sign), :, cut]
        else:
            source = sum_x.at[slot, :, cut]
        return remote(
            source,
            land_x.at[slot, :, cut],
            x_send.at[slot, piece],
            x_recv.at[slot, piece],
            {"rep": rep_at(sign)},
        )

    for piece in range(PIECES):
        for route, _ in turns:
            x_copy(route, 0, piece).start()

    def ba_first(step, slot):
        to, where = flat_peer(step)
        return remote(
            ba_ref, land_ba.at[deep, slot], b_send.at[0, step], b_recv.at[0, slot], where
        )

    def bm_first(step, slot):
        to, where = flat_peer(step)
        return remote(
            bm_ref, land_bm.at[deep, slot], b_send.at[1, step], b_recv.at[1, slot], where
        )

    def ba_second(step, slot):
        to, where = deep_peer(step)
        return remote(
            land_ba.at[slot], land_ba.at[slot], c_send.at[0, step], c_recv.at[0, slot], where
        )

    def bm_second(step, slot):
        to, where = deep_peer(step)
        return remote(
            land_bm.at[slot], land_bm.at[slot], c_send.at[1, step], c_recv.at[1, slot], where
        )

    def small_copy(step, slot):
        return remote(
            sg_ref, land_sm.at[slot], sm_send.at[step], sm_recv.at[slot], {"rep": rep_at(step)}
        )

    @pl.loop(1, GROUP)
    def _(step):
        ba_first(step, flat).start()

    land_ba[deep, flat] = ba_ref[...]

    @pl.when(in_side)
    def _():
        @pl.loop(1, GROUP)
        def _(step):
            bm_first(step, near).start()

        land_bm[deep, near] = bm_ref[...]

    @pl.loop(1, reps)
    def _(step):
        small_copy(step, rep).start()

    land_sm[rep] = sg_ref[...]

    @pl.loop(1, GROUP)
    def _(step):
        ba_first(step, flat_peer(step)[0]).wait_recv()

    @pl.loop(0, 4)
    def _(slot):
        @pl.when(slot != near)
        def _():
            bm_first(1, slot).wait_recv()

    @pl.loop(1, GROUP)
    def _(step):
        ba_second(step, deep).start()
        bm_second(step, deep).start()

    for step in range(1, 4):
        for piece in range(PIECES):
            for route, steps in turns:
                if step < steps:
                    sign = way if route == 0 else -way
                    cut = cuts(width)[piece]
                    x_copy(route, step - 1, piece).wait_recv()
                    sum_x[4 * route + step, :, cut] = (
                        land_x[4 * route + step - 1, :, cut]
                        + x_ref[rep_at((steps - step) * sign), :, cut]
                    )
                    x_copy(route, step, piece).start()

    @pl.loop(1, GROUP)
    def _(step):
        ba_second(step, deep_peer(step)[0]).wait_recv()
        bm_second(step, deep_peer(step)[0]).wait_recv()

    @pl.loop(0, GROUP)
    def _(slot):
        for place in range(GROUP):
            lo = (place % 2) * rows
            basis_a[(place // 2) * GROUP + slot, lo : lo + rows, :] = land_ba[slot, place]
        for place in range(4):
            packed = land_bm[slot, place]
            for group in range(4):
                basis_m[
                    ((place // 2) * GROUP + slot) * 2 + place % 2,
                    group * rows : (group + 1) * rows,
                    :,
                ] = packed[:, group * rank : (group + 1) * rank]

    s_ref[...] = jnp.zeros_like(s_ref)
    for piece in range(PIECES):
        cut = cuts(width)[piece]
        for route, steps in turns:
            x_copy(route, steps - 1, piece).wait_recv()
        s_ref[0:rows, cut] = x_ref[rep, :, cut] + (land_x[3, :, cut] + land_x[6, :, cut])

    def swap(turn):
        return remote(
            swap_out.at[turn],
            swap_in.at[turn],
            swap_send.at[turn],
            swap_recv.at[turn],
            {"rep": pair},
        )

    def swap_begin(turn, term):
        swap_out[turn] = term
        swap(turn).start()

    def swap_end(turn, term):
        swap(turn).wait()
        return term + swap_in[turn]

    share = tiles // GROUP // PIECES
    span = width // PIECES
    blocks = span // LANES
    high = rank // TILE

    def columns(piece):
        return slice(piece * span, (piece + 1) * span)

    def right_round(turn, left_of, scale, use):
        def p_copy(piece, step, slot):
            to, where = flat_peer(step)
            return remote(
                part.at[turn, piece, to],
                land_p.at[turn, piece, slot],
                p_send.at[turn * PIECES + piece, step],
                p_recv.at[turn * PIECES + piece, slot],
                where,
            )

        def z_copy(piece, step, slot):
            to, where = deep_peer(step)
            return remote(
                part_z.at[turn, piece],
                land_z.at[turn, piece, slot],
                z_send.at[turn * PIECES + piece, step],
                z_recv.at[turn * PIECES + piece, slot],
                where,
            )

        def g_copy(piece, step, slot):
            to, where = flat_peer(step)
            return remote(
                full.at[turn, piece, slot],
                full.at[turn, piece, slot],
                g_send.at[turn * PIECES + piece, step],
                g_recv.at[turn * PIECES + piece, slot],
                where,
            )

        for piece in range(PIECES):
            value = dot_tn(left_of(piece), s_ref[:, columns(piece)])
            for block in range(blocks):
                for line in range(high):
                    tile = block * high + line
                    part[turn, piece, tile // share, tile % share] = value[
                        line * TILE : (line + 1) * TILE, block * LANES : (block + 1) * LANES
                    ]

            @pl.loop(1, GROUP)
            def _(step):
                p_copy(piece, step, flat).start()

            land_p[turn, piece, flat] = part[turn, piece, flat]

        for piece in range(PIECES):

            @pl.loop(1, GROUP)
            def _(step):
                p_copy(piece, step, flat_peer(step)[0]).wait_recv()

            part_z[turn, piece] = jnp.sum(land_p[turn, piece], axis=0)

            @pl.loop(1, GROUP)
            def _(step):
                z_copy(piece, step, deep).start()

            land_z[turn, piece, deep] = part_z[turn, piece]

        for piece in range(PIECES):

            @pl.loop(1, GROUP)
            def _(step):
                z_copy(piece, step, deep_peer(step)[0]).wait_recv()

            full[turn, piece, flat] = jnp.sum(land_z[turn, piece], axis=0) * scale

            @pl.loop(1, GROUP)
            def _(step):
                g_copy(piece, step, flat).start()

        for piece in range(PIECES):

            @pl.loop(1, GROUP)
            def _(step):
                g_copy(piece, step, flat_peer(step)[0]).wait_recv()

            whole = full[turn, piece].reshape(tiles // PIECES, TILE, LANES)
            use(
                piece,
                jnp.concatenate(
                    [
                        whole[block * high : (block + 1) * high].reshape(rank, LANES)
                        for block in range(blocks)
                    ],
                    axis=1,
                ),
            )

        for piece in range(PIECES):

            @pl.loop(1, GROUP)
            def _(step):
                p_copy(piece, step, flat).wait_send()
                z_copy(piece, step, deep).wait_send()
                g_copy(piece, step, flat).wait_send()

    def once(make_a, make_m):
        held = []

        def left_of(piece):
            if piece == 0:
                held.append(make_a())
            elif piece == 1:
                held.append(make_m())
            return held[min(piece, 1)]

        return held, left_of

    basis_full_a = basis_a[...].reshape(cols_a, rank)
    basis_full_m = basis_m[...].reshape(cols_m, rank)
    first_m = dot_nn(s_ref[:, cols_a:width], basis_full_m)
    swap_begin(0, first_m)

    seconds = []
    right_round(
        0,
        once(
            lambda: dot_nn(dot_nn(s_ref[:, 0:cols_a], basis_full_a), ar_ref[rep, 0]),
            lambda: dot_nn(swap_end(0, first_m), mr_ref[rep // 2, 0]),
        )[1],
        1.0,
        lambda piece, right: seconds.append(dot_nt(s_ref[:, columns(piece)], right)),
    )
    second_m = seconds[1] + seconds[2]
    swap_begin(1, second_m)

    y_edges = [0, span, 2 * span, wide]

    def y_cut(piece):
        return slice(y_edges[piece], y_edges[piece + 1])

    def y_copy(route, step, piece):
        sign = way if route == 0 else -way
        block = y_ref.at[rep_at(-step * sign), :, y_cut(piece)]
        slot = 4 * route + step
        return remote(
            block, block, y_send.at[slot, piece], y_recv.at[slot, piece], {"rep": rep_at(sign)}
        )

    def y_landed(route, step, piece):
        sign = way if route == 0 else -way
        block = y_ref.at[rep_at(-(step + 1) * sign), :, y_cut(piece)]
        slot = 4 * route + step
        return remote(
            block, block, y_send.at[slot, piece], y_recv.at[slot, piece], {"rep": rep_at(sign)}
        )

    rights = []
    lefts, left_of = once(
        lambda: dot_nn(dot_nn(seconds[0], ar_ref[rep, 1]), ar_ref[rep, 2]),
        lambda: dot_nn(
            dot_nn(swap_end(1, second_m), mr_ref[rep // 2, 1]), mr_ref[rep // 2, 2]
        ),
    )

    def send_approx(piece, right):
        rights.append(right)
        y_ref[rep, :, columns(piece)] = dot_nn(lefts[min(piece, 1)], right)[0:rows]
        if piece < PIECES - 1:
            for route, _ in turns:
                y_copy(route, 0, piece).start()

    right_round(1, left_of, 1.0 / reps, send_approx)
    left_a, left_m = lefts
    right_a, right_m = rights[0], jnp.concatenate(rights[1:], axis=1)
    padded = left_a.shape[0]
    line = lax.broadcasted_iota(jnp.int32, (padded, cols_a), 0)
    column = lax.broadcasted_iota(jnp.int32, (padded, cols_a), 1)
    pick_a = jnp.where(column == me * rows + line, 1.0, 0.0).astype(jnp.float32)
    line = lax.broadcasted_iota(jnp.int32, (padded, cols_m), 0)
    column = lax.broadcasted_iota(jnp.int32, (padded, cols_m), 1)
    factors = [left_a, left_m, dot_nt(pick_a, right_a)]
    for group in range(4):
        start = (me - side * (shards // 2)) * (4 * rows) + group * rows
        pick_m = jnp.where(column == start + line, 1.0, 0.0).astype(jnp.float32)
        factors.append(dot_nt(pick_m, right_m))
    factors.append(jnp.zeros_like(left_a))
    for at, factor in enumerate(factors):
        lo = width + at * rank
        y_ref[rep, :, lo : lo + rank] = factor[0:rows]
    for route, _ in turns:
        y_copy(route, 0, PIECES - 1).start()

    for step in range(1, 4):
        for piece in range(PIECES):
            for route, steps in turns:
                if step < steps:
                    y_landed(route, step - 1, piece).wait_recv()
                    y_copy(route, step, piece).start()

    @pl.loop(1, reps)
    def _(step):
        small_copy(step, rep_at(step)).wait_recv()

    total = land_sm[0]
    for slot in range(1, reps):
        total = total + land_sm[slot]
    small_ref[...] = total

    @pl.loop(1, GROUP)
    def _(step):
        ba_first(step, flat).wait_send()
        ba_second(step, deep).wait_send()
        bm_second(step, deep).wait_send()

    @pl.when(in_side)
    def _():
        @pl.loop(1, GROUP)
        def _(step):
            bm_first(step, near).wait_send()

    @pl.loop(1, reps)
    def _(step):
        small_copy(step, rep).wait_send()

    for route, steps in turns:
        for piece in range(PIECES):
            y_landed(route, steps - 1, piece).wait_recv()
            for step in range(steps):
                x_copy(route, step, piece).wait_send()
                y_copy(route, step, piece).wait_send()


def power_call(shape, *operands):
    shards, reps, rows, cols_a, cols_m, rank, tiles = shape
    padded = 16
    width = cols_a + cols_m
    wide = width + 8 * rank
    share = tiles // GROUP // PIECES
    assert shards == GROUP * GROUP and reps == GROUP
    assert tiles == share * GROUP * PIECES and width == PIECES * cols_a
    f32 = jnp.float32
    vmem = pl.BlockSpec(memory_space=pltpu.VMEM)
    dma = pltpu.SemaphoreType.DMA
    layers, entries = operands[-1].shape
    small = (layers, -(-entries // LANES) * LANES)

    def body(*refs):
        power_kernel(shape, *refs)

    return pl.pallas_call(
        body,
        out_shape=(
            jax.ShapeDtypeStruct((reps, rows, wide), f32),
            jax.ShapeDtypeStruct(small, f32),
        ),
        in_specs=[vmem] * len(operands),
        out_specs=(vmem, vmem),
        scratch_shapes=[
            pltpu.VMEM((reps, rows, width), f32),
            pltpu.VMEM((rows, rank), f32),
            pltpu.VMEM((rows, 4 * rank), f32),
            pltpu.VMEM(small, f32),
            pltpu.VMEM((7, rows, width), f32),
            pltpu.VMEM((7, rows, width), f32),
            pltpu.VMEM((padded, width), f32),
            pltpu.VMEM((GROUP, GROUP, rows, rank), f32),
            pltpu.VMEM((GROUP, 4, rows, 4 * rank), f32),
            pltpu.VMEM((shards // 2, 2 * rows, rank), f32),
            pltpu.VMEM((shards // 2, 4 * rows, rank), f32),
            pltpu.VMEM((reps,) + small, f32),
            pltpu.VMEM((2, padded, rank), f32),
            pltpu.VMEM((2, padded, rank), f32),
            pltpu.VMEM((2, PIECES, GROUP, share, TILE, LANES), f32),
            pltpu.VMEM((2, PIECES, GROUP, share, TILE, LANES), f32),
            pltpu.VMEM((2, PIECES, share, TILE, LANES), f32),
            pltpu.VMEM((2, PIECES, GROUP, share, TILE, LANES), f32),
            pltpu.VMEM((2, PIECES, GROUP, share, TILE, LANES), f32),
        ]
        + [dma((7, PIECES))] * 4
        + [dma((reps,))] * 2
        + [dma((2, GROUP))] * 4
        + [dma((2,))] * 2
        + [dma((2 * PIECES, GROUP))] * 6,
        compiler_params=pltpu.CompilerParams(collective_id=0, has_side_effects=True),
        name="power_rounds",
    )(*operands)


def update_kernel(
    shape,
    y_ref,
    small_ref,
    ag_ref,
    ae_ref,
    am_ref,
    aw_ref,
    mg_ref,
    me_ref,
    mm_ref,
    mw_ref,
    sm_ref,
    sw_ref,
    ae_out,
    me_out,
    al_out,
    ar_out,
    ml_out,
    mr_out,
    am_out,
    aw_out,
    mm_out,
    mw_out,
    sm_out,
    sw_out,
    turned,
):
    shards, reps, rows, cols_a, cols_m, rank, tiles = shape
    width = cols_a + cols_m
    layers, kinds_a, kinds_m = ag_ref.shape[0], ag_ref.shape[2], mg_ref.shape[2]

    def finish(grad, error, momentum, weights, approx):
        stepped = momentum_decay * momentum + approx
        return (
            grad.astype(jnp.float32) + error - approx,
            stepped,
            weights - learn_rate * stepped,
        )

    def lanes(at):
        return slice(width + at * rank, width + (at + 1) * rank)

    for layer in range(layers):
        for row in range(rows):
            lo = layer * kinds_a
            approx = y_ref[lo : lo + kinds_a, row, 0:cols_a]
            ae_out[layer, row], am_out[layer, row], aw_out[layer, row] = finish(
                ag_ref[layer, row],
                ae_ref[layer, row],
                am_ref[layer, row],
                aw_ref[layer, row],
                approx,
            )
            al_out[layer, row] = y_ref[lo : lo + kinds_a, row, lanes(0)]
            ar_out[layer, row] = y_ref[lo : lo + kinds_a, row, lanes(2)]
            first = [(layer * kinds_m + kind) * 2 for kind in range(kinds_m)]
            approx = jnp.concatenate(
                [
                    jnp.concatenate(
                        [y_ref[at, row : row + 1, cols_a:width] for at in (one, one + 1)], axis=1
                    )
                    for one in first
                ],
                axis=0,
            )
            me_out[layer, row], mm_out[layer, row], mw_out[layer, row] = finish(
                mg_ref[layer, row],
                me_ref[layer, row],
                mm_ref[layer, row],
                mw_ref[layer, row],
                approx,
            )
            for kind in range(kinds_m):
                ml_out[layer, row, kind : kind + 1] = y_ref[first[kind], row : row + 1, lanes(1)]
        for kind in range(kinds_m):
            one = (layer * kinds_m + kind) * 2
            for group in range(4):
                turned[group * rows : (group + 1) * rows] = (
                    y_ref[one, :, lanes(3 + group)] + y_ref[one + 1, :, lanes(3 + group)]
                )
            mr_out[layer, kind] = turned[...].T
    entries = sm_ref.shape[1]
    mean = small_ref[:, 0:entries] / float(reps)
    stepped = momentum_decay * sm_ref[...] + mean
    sm_out[...] = stepped
    sw_out[...] = sw_ref[...] - learn_rate * stepped


def update_call(shape, *operands):
    shards, reps, rows, cols_a, cols_m, rank, tiles = shape
    f32 = jnp.float32
    attn, mlp, small = operands[3].shape, operands[7].shape, operands[-1].shape
    layers, kinds_a, kinds_m = attn[0], attn[2], mlp[2]
    vmem = pl.BlockSpec(memory_space=pltpu.VMEM)

    def body(*refs):
        update_kernel(shape, *refs)

    shapes = [
        attn,
        mlp,
        (layers, rows, kinds_a, rank),
        (layers, rows, kinds_a, rank),
        (layers, rows, kinds_m, rank),
        (layers, kinds_m, rank, 4 * rows),
        attn,
        attn,
        mlp,
        mlp,
        small,
        small,
    ]
    return pl.pallas_call(
        body,
        out_shape=tuple(jax.ShapeDtypeStruct(each, f32) for each in shapes),
        in_specs=[vmem] * len(operands),
        out_specs=(vmem,) * len(shapes),
        scratch_shapes=[pltpu.VMEM((4 * rows, rank), f32)],
        name="apply_update",
    )(*operands)


def per_device(
    attn_grad,
    attn_error,
    attn_basis,
    attn_roots,
    attn_momentum,
    attn_weights,
    mlp_grad,
    mlp_error,
    mlp_basis,
    mlp_roots,
    mlp_momentum,
    mlp_weights,
    small_grad,
    small_momentum,
    small_weights,
):
    shards, reps = lax.axis_size("shard"), lax.axis_size("rep")
    layers, kinds_a, rows, cols_a = attn_error.shape[1:]
    kinds_m, _, columns_m = mlp_error.shape[2:]
    rank = attn_basis.shape[-1]
    mats_a, mats_m = layers * kinds_a, layers * kinds_m
    cols_m = columns_m // 2
    assert mats_a == reps and 2 * mats_m == reps
    tiles = (cols_a + cols_m) * rank // (TILE * LANES)
    shape = (shards, reps, rows, cols_a, cols_m, rank, tiles)

    def flip(array):
        return array.transpose(0, 2, 1, 3)

    ag, ae = flip(attn_grad[0]), flip(attn_error[0])
    mg, me = flip(mlp_grad[0]), flip(mlp_error[0])
    y, small = power_call(
        shape,
        ag,
        ae,
        mg,
        me,
        flip(attn_basis),
        mlp_basis.transpose(0, 1, 3, 2),
        attn_roots.reshape(mats_a, 3, rank, rank),
        mlp_roots.reshape(mats_m, 3, rank, rank),
        small_grad[0],
    )
    outs = update_call(
        shape,
        y,
        small,
        ag,
        ae,
        flip(attn_momentum),
        flip(attn_weights),
        mg,
        me,
        flip(mlp_momentum),
        flip(mlp_weights),
        small_momentum,
        small_weights,
    )
    return (
        flip(outs[0])[None],
        flip(outs[1])[None],
        flip(outs[2]),
        flip(outs[3]),
        flip(outs[4]),
        outs[5].transpose(0, 1, 3, 2),
        flip(outs[6]),
        flip(outs[7]),
        flip(outs[8]),
        flip(outs[9]),
        outs[10],
        outs[11],
    )


def solution(mesh):
    in_specs = (
        P("rep", None, None, "shard", None),
        P("rep", None, None, "shard", None),
        P(None, None, "shard", None),
        P(),
        P(None, None, "shard", None),
        P(None, None, "shard", None),
        P("rep", None, None, "shard", None),
        P("rep", None, None, "shard", None),
        P(None, None, "shard", None),
        P(),
        P(None, None, "shard", None),
        P(None, None, "shard", None),
        P("rep", None, "shard"),
        P(None, "shard"),
        P(None, "shard"),
    )
    out_specs = (
        P("rep", None, None, "shard", None),
        P("rep", None, None, "shard", None),
        P(None, None, "shard", None),
        P(None, None, "shard", None),
        P(None, None, "shard", None),
        P(None, None, "shard", None),
        P(None, None, "shard", None),
        P(None, None, "shard", None),
        P(None, None, "shard", None),
        P(None, None, "shard", None),
        P(None, "shard"),
        P(None, "shard"),
    )
    return jax.shard_map(
        per_device, mesh=mesh, in_specs=in_specs, out_specs=out_specs, check_vma=False
    )
```
